128 devices in a mesh: row: 8 (over x_lo, z), col: 16 (over x_hi, y, core).
Axes of the slice: x: 4 (x_hi: 2, x_lo: 2; x = x_hi * 2 + x_lo), y: 4, z: 4, core: 2. Of those that a mesh axis runs over, the one named last changes fastest.
Arguments:
- hessian: float32 [18432, 18432], P('row', 'col'), may hold values from -1 to 5, as said below
- right_side: float32 [18432, 512], P('row'), may hold values from -6 to 6
- mask: int32 [18432, 512], P('row'), may hold values 0 or 1
- damping: float32 [1], replicated, may hold values from 0.4 to 1.2
Outputs:
- solution: float32 [18432, 512], P('row')
The draws below stay inside these ranges and needn't reach their ends.
Inputs may be any that keep to these rules, and one draw needn't show every extreme that they name: hessian is symmetric and positive definite.
All inputs are finite; a program needn't handle non-finite values. No bound on the sum of `mask` on one device may be relied on, other than what follows from the above.
Results may differ from the reference program's by a relative error of at most 0.0001.
Values sent between devices are 32-bit elements; how exact they have to be, the bound alone decides.
A program may use at most 128 MiB of HBM per device.

```python
import math
import jax
import jax.numpy as jnp
from jax import lax

ORDER = 18432
COLS = 512
ITERS = 3


def draw_hessian(key, part):
    key_noise, key_diagonal = jax.random.split(jax.random.fold_in(key, 11))
    spread = 0.5 / math.sqrt(ORDER)
    noise_field = jax.random.normal(key_noise, (ORDER, ORDER), jnp.float32)
    symmetric = (noise_field + noise_field.T) * (spread * 0.70710678)
    diagonal = jnp.exp(jax.random.uniform(key_diagonal, (ORDER,), jnp.float32, math.log(0.8), math.log(5.0)))
    positions = jnp.arange(ORDER)
    return symmetric.at[positions, positions].set(diagonal)


def place_ends(drawn, key, low, top_value):
    place = [jax.random.randint(jax.random.fold_in(key, axis), (), 0, length) for axis, length in enumerate(drawn.shape)]
    main_axis = drawn.shape.index(max(drawn.shape))
    next_to = place[:main_axis] + [(place[main_axis] + 1) % drawn.shape[main_axis]] + place[main_axis + 1:]
    return drawn.at[tuple(place)].set(low).at[tuple(next_to)].set(top_value)


def level_of(rng, shape, pieces, least, top_value):
    def one(axis_at, blocks):
        draws = jax.random.uniform(jax.random.fold_in(jax.random.fold_in(rng, 6), axis_at), (blocks,), jnp.float32, least / len(pieces), top_value / len(pieces))
        return jnp.repeat(jnp.exp(draws), shape[axis_at] // blocks).reshape((-1,) + (1,) * (len(shape) - axis_at - 1))

    level = one(*pieces[0])
    for cut in pieces[1:]:
        level = level * one(*cut)
    return level


def bell_draw(stream_key, shape, deviation, most, cuts=(), held_as=jnp.bfloat16):
    values = jax.random.normal(stream_key, shape, jnp.float32) * deviation
    if len(cuts) > 0:
        values = level_of(stream_key, shape, cuts, -0.22, 0.18) * values
    return jnp.clip(values, min=-most, max=most).astype(held_as)


def setup_inputs(seed: int = 0) -> dict:
    key_list = jax.random.split(jax.random.key(seed), 5)
    return {
        "hessian": draw_hessian(jax.random.fold_in(key_list[4], 71), 0),
        "right_side": bell_draw(key_list[1], (ORDER, COLS), 1.0, 6.0, ((0, 8),), jnp.float32),
        "mask": place_ends((jax.random.randint(key_list[2], (ORDER, COLS), 0, 4) < 3).astype(jnp.int32), jax.random.fold_in(key_list[2], 1), 0, 1),
        "damping": jnp.clip(jnp.exp(jax.random.uniform(key_list[3], (1,), jnp.float32, math.log(0.4), math.log(1.2))), 0.4, 1.2),
    }


epsilon = 1e-6


def reference(hessian, right_side, mask, damping):
    mask_float = mask.astype(jnp.float32)
    damping_value = damping[0]

    def masked_apply(vector):
        product = jnp.dot(hessian, vector, precision=lax.Precision.HIGHEST, preferred_element_type=jnp.float32)
        return mask_float * (product + damping_value * vector)

    residual = mask_float * right_side
    direction = residual
    solution = jnp.zeros_like(right_side)
    norm_now = jnp.sum(residual * residual, axis=0)
    for iteration in range(ITERS):
        applied = masked_apply(direction)
        curvature = jnp.sum(direction * applied, axis=0)
        step_size = norm_now / (curvature + epsilon)
        solution = solution + step_size * direction
        residual = residual - step_size * applied
        norm_next = jnp.sum(residual * residual, axis=0)
        direction = residual + (norm_next / (norm_now + epsilon)) * direction
        norm_now = norm_next
    return solution
```

```python
import jax
import jax.numpy as jnp
from jax import lax
from jax.experimental import pallas as pl
from jax.experimental.pallas import tpu as pltpu
from jax.sharding import PartitionSpec as P

MESH = pl.DeviceIdType.MESH
F32 = jnp.float32
BF16 = jnp.bfloat16

epsilon = 1e-06

SHARD = 144
QUARTER = 2 * SHARD
WIDTH = 8 * SHARD
ROWS = 16 * SHARD
BLOCK = 4 * SHARD
DEPTH = 256
DEPTHS = ROWS // DEPTH
GROUPS = 2
COPIES = 40
SUMS = 3
PEERS = 10


def halves(value):
    high = value.astype(BF16)
    return high, (value - high.astype(F32)).astype(BF16)


def dot3(a_high, a_low, b_high, b_low, contract):
    dims = ((contract, (0,)), ((), ()))

    def one(a, b):
        return lax.dot_general(a, b, dims, preferred_element_type=F32)

    return one(a_high, b_high) + (one(a_high, b_low) + one(a_low, b_high))


def column_sum(a, b):
    return jnp.sum(a * b, axis=0, keepdims=True)


class Copies:
    def __init__(self, send, receive):
        self.send, self.receive, self.used = send, receive, 0

    def to(self, source, target, device):
        k = self.used
        self.used += 1
        copy = pltpu.make_async_remote_copy(
            src_ref=source,
            dst_ref=target,
            send_sem=self.send.at[k],
            recv_sem=self.receive.at[k],
            device_id=device,
            device_id_type=MESH,
        )
        copy.start()
        return copy


class ToTwin:
    def __init__(self, copies, source, target, place):
        k = copies.used
        copies.used += 1
        self.alone = place["alone"]
        self.remote = pltpu.make_async_remote_copy(
            src_ref=source,
            dst_ref=target,
            send_sem=copies.send.at[k],
            recv_sem=copies.receive.at[k],
            device_id=place["twin"],
            device_id_type=MESH,
        )
        self.local = pltpu.make_async_copy(source, target, copies.receive.at[k])

        @pl.when(self.alone)
        def _():
            self.local.start()

        @pl.when(jnp.logical_not(self.alone))
        def _():
            self.remote.start()

    def wait(self):
        @pl.when(self.alone)
        def _():
            self.local.wait()

        @pl.when(jnp.logical_not(self.alone))
        def _():
            self.remote.wait()


def find_place():
    row, col = lax.axis_index("row"), lax.axis_index("col")
    x_low, z = lax.div(row, 4), lax.rem(row, 4)
    x_high, y, core = lax.div(col, 8), lax.rem(lax.div(col, 2), 4), lax.rem(col, 2)
    row_x, col_x = lax.rem(row + 4, 8), lax.rem(col + 8, 16)
    place = dict(x_low=x_low, z=z, x_high=x_high, y=y, core=core)
    place["z_peers"] = [(x_low * 4 + lax.rem(z + d, 4), col) for d in (1, 2, 3)]
    place["y_peers"] = [(row, x_high * 8 + lax.rem(y + d, 4) * 2 + core) for d in (1, 2, 3)]
    place["x_low_peer"] = (row_x, col)
    place["x_high_peer"] = (row, col_x)
    place["x_peers"] = [(row_x, col), (row, col_x), (row_x, col_x)]
    place["core_peer"] = (row, col + 1 - 2 * core)
    place["twin"] = (x_high * 4 + y, x_low * 8 + z * 2 + core)
    place["alone"] = jnp.logical_and(x_low == x_high, z == y)
    return place


def kernel(
    h_hbm, b_hbm, mask_hbm, damping_ref, out_hbm,
    h_stage, h_high, h_low, mask, r0, r1_rows, r2_rows, cols1, cols2,
    part0, part1, got_z, got_x, got_core, got_y, got_x2, send_x, send_x2,
    r0_own, mask_own, mask_sent, w0_own, w0_rows, w1_rows,
    v_high, v_low, tile_out, tile_in, stage_sem, in_sem, out_sem, send_sem, receive_sem,
):
    groups, _, width = r0.shape
    place = find_place()
    z, y, core, x_low, x_high = (place[k] for k in ("z", "y", "core", "x_low", "x_high"))
    damping = damping_ref[0]

    def load(k, slot):
        return pltpu.make_async_copy(
            h_hbm.at[pl.ds(k * DEPTH, DEPTH), :], h_stage.at[slot], stage_sem.at[slot]
        )

    loads = []
    for g in range(groups):
        columns = pl.ds(g * width, width)
        loads.append(
            (
                pltpu.make_async_copy(b_hbm.at[:, columns], r0.at[g], in_sem.at[2 * g]),
                pltpu.make_async_copy(mask_hbm.at[:, columns], mask.at[g], in_sem.at[2 * g + 1]),
            )
        )
    for pair in loads[:1]:
        for copy in pair:
            copy.start()
    load(0, 0).start()
    load(1, 1).start()
    for pair in loads[1:]:
        for copy in pair:
            copy.start()

    barrier = pltpu.get_barrier_semaphore()
    peers = [*place["z_peers"], *place["y_peers"], *place["x_peers"], place["core_peer"]]
    for peer in peers:
        pl.semaphore_signal(barrier, inc=1, device_id=peer, device_id_type=MESH)

    @pl.when(jnp.logical_not(place["alone"]))
    def _():
        pl.semaphore_signal(barrier, inc=1, device_id=place["twin"], device_id_type=MESH)
        pl.semaphore_wait(barrier, len(peers) + 1)

    @pl.when(place["alone"])
    def _():
        pl.semaphore_wait(barrier, len(peers))

    row_at = pl.multiple_of(core * WIDTH + y * QUARTER + x_high * SHARD, 8)
    col_at = pl.multiple_of(z * QUARTER + x_low * SHARD, 8)
    row_own, col_own = pl.ds(row_at, SHARD), pl.ds(col_at, SHARD)
    twin_own = pl.ds(pl.multiple_of(y * QUARTER + x_high * SHARD, 8), SHARD)
    mine, others = pl.multiple_of(core * WIDTH, 8), pl.multiple_of((1 - core) * WIDTH, 8)

    def first_rows(g):
        @pl.loop(0, 8)
        def _(k):
            at = pl.ds(pl.multiple_of(k * QUARTER, 8), QUARTER)
            r0[g, at, :] = r0[g, at, :] * mask[g, at, :].astype(F32)

    def multiply_first(g, fresh):
        part0[g] = jnp.zeros_like(part0[g])

        @pl.loop(0, DEPTHS)
        def _(k):
            at = pl.ds(pl.multiple_of(k * DEPTH, DEPTH), DEPTH)
            if fresh:
                slot = lax.rem(k, 2)
                load(k, slot).wait()
                high, low = halves(h_stage[slot])
                h_high[at, :] = high
                h_low[at, :] = low

                @pl.when(k < DEPTHS - 2)
                def _():
                    load(k + 2, slot).start()
            b_high, b_low = halves(r0[g, at, :])
            part0[g] += dot3(h_high[at, :], h_low[at, :], b_high, b_low, (0,))

    def split_columns(source, g):
        @pl.loop(0, 4)
        def _(k):
            at = pl.ds(pl.multiple_of(k * QUARTER, 16), QUARTER)
            high, low = halves(source[g, at, :])
            v_high[g, at, :] = high
            v_low[g, at, :] = low

    def multiply_rows(at, g):
        return dot3(h_high[at, :], h_low[at, :], v_high[g], v_low[g], (1,))

    def all_sums(copies, g, s, values):
        lines = width // 128
        steps = ([place["core_peer"]], place["z_peers"], place["y_peers"], place["x_peers"])
        tile_out[g, s, 0] = jnp.zeros((8, 128), F32)
        for v, value in enumerate(values):
            for l in range(lines):
                tile_out[g, s, 0, pl.ds(v * lines + l, 1), :] = value[:, l * 128:(l + 1) * 128]
        slot = 0
        for step, group in enumerate(steps):
            sent = []
            for peer in group:
                sent.append(copies.to(tile_out.at[g, s, step], tile_in.at[g, s, slot], peer))
                slot += 1
            yield
            for copy in sent:
                copy.wait()
            total = tile_out[g, s, step]
            for k in range(slot - len(sent), slot):
                total = total + tile_in[g, s, k]
            if step + 1 < len(steps):
                tile_out[g, s, step + 1] = total
        result = []
        for v in range(len(values)):
            result.append(
                jnp.concatenate([total[v * lines + l:v * lines + l + 1, :] for l in range(lines)], axis=1)
            )
        return result

    def reduce_by(copies, g, source, start, got, quarter, peers_, sent_x, got_last, half, x_peer):
        sent = []
        for d in range(3):
            at = pl.multiple_of(start + lax.rem(quarter + d + 1, 4) * QUARTER, 8)
            sent.append(copies.to(source.at[g, pl.ds(at, QUARTER), :], got.at[g, d], peers_[d]))
        yield
        for copy in sent:
            copy.wait()

        def added(which):
            inner = pl.ds(pl.multiple_of(which * SHARD, 8), SHARD)
            at = pl.ds(pl.multiple_of(start + quarter * QUARTER + which * SHARD, 8), SHARD)
            return (source[g, at, :] + got[g, 0, inner, :]) + (got[g, 1, inner, :] + got[g, 2, inner, :])

        sent_x[g] = added(1 - half)
        last = copies.to(sent_x.at[g], got_last.at[g], x_peer)
        own = added(half)
        yield
        last.wait()
        return own + got_last[g]

    def gather_by(copies, g, whole, own, start, x_peer, peers_):
        first = copies.to(whole.at[g, own, :], whole.at[g, own, :], x_peer)
        yield
        first.wait()
        at = pl.ds(start, QUARTER)
        sent = [copies.to(whole.at[g, at, :], whole.at[g, at, :], peer) for peer in peers_]
        yield
        for copy in sent:
            copy.wait()

    def gather_rows(copies, g, whole):
        start = pl.multiple_of(core * WIDTH + y * QUARTER, 8)
        yield from gather_by(copies, g, whole, row_own, start, place["x_high_peer"], place["y_peers"])
        at = pl.ds(mine, WIDTH)
        last = copies.to(whole.at[g, at, :], whole.at[g, at, :], place["core_peer"])
        yield
        last.wait()

    def gather_columns(copies, g, whole):
        start = pl.multiple_of(z * QUARTER, 8)
        yield from gather_by(copies, g, whole, col_own, start, place["x_low_peer"], place["z_peers"])

    def both(first, second):
        going = [first, second]
        while going:
            for one in list(going):
                try:
                    next(one)
                except StopIteration:
                    going.remove(one)
            if going:
                yield

    def group(g):
        copies = Copies(send_sem.at[g], receive_sem.at[g])
        for copy in loads[g]:
            copy.wait()
        first_rows(g)
        mask_sent[g] = mask[g, row_own, :].astype(F32)
        r0_moved = ToTwin(copies, r0.at[g, row_own, :], r0_own.at[g], place)
        mask_moved = ToTwin(copies, mask_sent.at[g], mask_own.at[g], place)
        multiply_first(g, g == 0)

        summed = yield from reduce_by(
            copies, g, part0, 0, got_z, z, place["z_peers"], send_x, got_x, x_low, place["x_low_peer"]
        )
        r0_moved.wait()
        mask_moved.wait()
        w0_own[g] = mask_own[g] * (summed + damping * r0_own[g])
        w0_moved = ToTwin(copies, w0_own.at[g], w0_rows.at[g], place)
        norm0, curve0 = yield from all_sums(
            copies, g, 0, [column_sum(r0_own[g], r0_own[g]), column_sum(r0_own[g], w0_own[g])]
        )
        step0 = norm0 / (curve0 + epsilon)
        cols1[g, col_own, :] = r0_own[g] - step0 * w0_own[g]
        w0_moved.wait()
        r1 = r0[g, row_own, :] - step0 * w0_rows[g]
        r1_rows[g, row_own, :] = r1

        rest = gather_rows(copies, g, r1_rows)
        column_side = gather_columns(copies, g, cols1)
        for _ in column_side:
            next(rest, None)
            yield
        split_columns(cols1, g)

        for half in (others, mine):
            @pl.loop(0, 2)
            def _(k):
                at = pl.ds(pl.multiple_of(half + k * BLOCK, 16), BLOCK)
                part1[g, at, :] = multiply_rows(at, g)
            if half is others:
                at = pl.ds(others, WIDTH)
                swapped = copies.to(part1.at[g, at, :], got_core.at[g], place["core_peer"])
        yield
        swapped.wait()

        @pl.loop(0, 4)
        def _(k):
            at = pl.ds(pl.multiple_of(mine + k * QUARTER, 8), QUARTER)
            inner = pl.ds(pl.multiple_of(k * QUARTER, 8), QUARTER)
            part1[g, at, :] = part1[g, at, :] + got_core[g, inner, :]

        summed = yield from reduce_by(
            copies, g, part1, mine, got_y, y, place["y_peers"], send_x2, got_x2, x_high, place["x_high_peer"]
        )
        for _ in rest:
            yield
        r1, w0 = r1_rows[g, row_own, :], w0_rows[g]
        w1_rows[g] = mask[g, row_own, :].astype(F32) * (summed + damping * r1)
        norm1, inner1, cross1 = yield from all_sums(
            copies, g, 1, [column_sum(r1, r1), column_sum(r1, w1_rows[g]), column_sum(r1, w0)]
        )
        ratio0 = norm1 / (norm0 + epsilon)
        curve1 = inner1 + ratio0 * (2.0 * cross1 + ratio0 * curve0)
        step1 = norm1 / (curve1 + epsilon)
        along = w1_rows[g] + ratio0 * w0_rows[g]
        r2 = r1_rows[g, row_own, :] - step1 * along
        r2_rows[g, row_own, :] = r2
        norm2, cross2 = column_sum(r2, r2), column_sum(r2, along)
        moved = ToTwin(copies, r2_rows.at[g, row_own, :], cols2.at[g, twin_own, :], place)
        rest = gather_rows(copies, g, r2_rows)
        next(rest, None)
        yield
        moved.wait()
        column_side = gather_columns(copies, g, cols2)
        for _ in column_side:
            next(rest, None)
            yield
        split_columns(cols2, g)

        def dotted(k, total, start):
            at = pl.ds(pl.multiple_of(start + k * BLOCK, 16), BLOCK)
            return total + column_sum(r2_rows[g, at, :], multiply_rows(at, g))

        for _ in rest:
            yield
        inner2 = lax.fori_loop(0, 4, lambda k, total: dotted(k, total, 0), jnp.zeros((1, width), F32))
        norm2, cross2, inner2 = yield from all_sums(copies, g, 2, [norm2, cross2, inner2])
        ratio1 = norm2 / (norm1 + epsilon)
        curve2 = (inner2 + damping * norm2) + ratio1 * (2.0 * cross2 + ratio1 * curve1)
        step2 = norm2 / (curve2 + epsilon)
        on_d1 = step1 + step2 * ratio1

        @pl.loop(0, 8)
        def _(k):
            at = pl.ds(pl.multiple_of(k * QUARTER, 8), QUARTER)
            first = r0[g, at, :]
            d1 = r1_rows[g, at, :] + ratio0 * first
            r0[g, at, :] = step0 * first + on_d1 * d1 + step2 * r2_rows[g, at, :]

        done = pltpu.make_async_copy(r0.at[g], out_hbm.at[:, pl.ds(g * width, width)], out_sem.at[g])
        done.start()
        yield
        done.wait()
        assert copies.used <= COPIES + SUMS * PEERS

    going = [group(g) for g in range(groups)]
    while going:
        for one in list(going):
            try:
                next(one)
            except StopIteration:
                going.remove(one)


def on_device(hessian, right_side, mask, damping):
    rows, columns = right_side.shape
    n, width = GROUPS, columns // GROUPS
    copies = COPIES + SUMS * PEERS

    def many(*shape, dtype=F32):
        return pltpu.VMEM((n, *shape, width), dtype)

    anywhere = pl.BlockSpec(memory_space=pl.ANY)
    return pl.pallas_call(
        kernel,
        out_shape=jax.ShapeDtypeStruct((rows, columns), F32),
        in_specs=[anywhere] * 3 + [pl.BlockSpec(memory_space=pltpu.SMEM)],
        out_specs=anywhere,
        scratch_shapes=[
            pltpu.VMEM((2, DEPTH, WIDTH), F32),
            pltpu.VMEM((ROWS, WIDTH), BF16),
            pltpu.VMEM((ROWS, WIDTH), BF16),
            many(ROWS, dtype=jnp.int32),
            many(ROWS), many(ROWS), many(ROWS), many(WIDTH), many(WIDTH),
            many(WIDTH), many(ROWS), many(3, QUARTER), many(SHARD), many(WIDTH), many(3, QUARTER), many(SHARD),
            many(SHARD), many(SHARD),
            many(SHARD), many(SHARD), many(SHARD), many(SHARD), many(SHARD), many(SHARD),
            many(WIDTH, dtype=BF16), many(WIDTH, dtype=BF16),
            pltpu.VMEM((n, SUMS, 4, 8, 128), F32),
            pltpu.VMEM((n, SUMS, PEERS, 8, 128), F32),
            pltpu.SemaphoreType.DMA((2,)),
            pltpu.SemaphoreType.DMA((2 * n,)),
            pltpu.SemaphoreType.DMA((n,)),
            pltpu.SemaphoreType.DMA((n, copies)),
            pltpu.SemaphoreType.DMA((n, copies)),
        ],
        compiler_params=pltpu.CompilerParams(
            collective_id=0, has_side_effects=True, vmem_limit_bytes=63 << 20
        ),
    )(hessian, right_side, mask, damping)


def solution(mesh):
    in_specs = (P("row", "col"), P("row", None), P("row", None), P())
    return jax.shard_map(
        on_device, mesh=mesh, in_specs=in_specs, out_specs=P("row", None), check_vma=False
    )
```

```python
import jax
import jax.numpy as jnp
from jax import lax
from jax.experimental import pallas as pl
from jax.experimental.pallas import tpu as pltpu
from jax.sharding import PartitionSpec as P

MESH = pl.DeviceIdType.MESH
F32 = jnp.float32
BF16 = jnp.bfloat16

epsilon = 1e-06

SHARD = 144
QUARTER = 2 * SHARD
WIDTH = 8 * SHARD
ROWS = 16 * SHARD
BLOCK = 4 * SHARD
DEPTH = 256
DEPTHS = ROWS // DEPTH
GROUPS = 2
COPIES = 48
SUMS = 5
NEAR = 7
FAR = 15


def halves(value):
    high = value.astype(BF16)
    return high, (value - high.astype(F32)).astype(BF16)


def dot3(a_high, a_low, b_high, b_low, contract):
    dims = ((contract, (0,)), ((), ()))

    def one(a, b):
        return lax.dot_general(a, b, dims, preferred_element_type=F32)

    return one(a_high, b_high) + (one(a_high, b_low) + one(a_low, b_high))


def column_sum(a, b):
    return jnp.sum(a * b, axis=0, keepdims=True)


class Copies:
    def __init__(self, send, receive):
        self.send, self.receive, self.used = send, receive, 0

    def to(self, source, target, device):
        k = self.used
        self.used += 1
        copy = pltpu.make_async_remote_copy(
            src_ref=source,
            dst_ref=target,
            send_sem=self.send.at[k],
            recv_sem=self.receive.at[k],
            device_id=device,
            device_id_type=MESH,
        )
        copy.start()
        return copy


class ToTwin:
    def __init__(self, copies, source, target, place):
        k = copies.used
        copies.used += 1
        self.alone = place["alone"]
        self.remote = pltpu.make_async_remote_copy(
            src_ref=source,
            dst_ref=target,
            send_sem=copies.send.at[k],
            recv_sem=copies.receive.at[k],
            device_id=place["twin"],
            device_id_type=MESH,
        )
        self.local = pltpu.make_async_copy(source, target, copies.receive.at[k])

        @pl.when(self.alone)
        def _():
            self.local.start()

        @pl.when(jnp.logical_not(self.alone))
        def _():
            self.remote.start()

    def wait(self):
        @pl.when(self.alone)
        def _():
            self.local.wait()

        @pl.when(jnp.logical_not(self.alone))
        def _():
            self.remote.wait()


def shard_at(start, ring, half):
    return pl.ds(pl.multiple_of(start + ring * QUARTER + half * SHARD, 8), SHARD)


class Reduce:
    def __init__(self, copies, part, relay, got, start, ring, half, device):
        self.copies, self.part, self.relay, self.got = copies, part, relay, got
        self.start, self.ring, self.half, self.device = start, ring, half, device

    def shard(self, step, flip):
        half = 1 - self.half if flip else self.half
        return shard_at(self.start, lax.rem(self.ring + step, 4), half)

    def send(self, step, flip, slot):
        at = self.shard(step, flip)
        return self.copies.to(self.part.at[at, :], self.got.at[slot], self.device(step, flip))

    def first(self):
        up = self.copies.to(self.part.at[self.shard(2, False), :], self.relay.at[0], self.device(1, False))
        down = self.copies.to(self.part.at[self.shard(2, True), :], self.relay.at[1], self.device(3, False))
        self.relays = [up, down]
        self.sent = [self.send(1, True, 1), self.send(3, False, 2), self.send(0, True, 4)]

    def second(self):
        for k, (step, flip) in enumerate(((1, False), (3, True))):
            self.relays[k].wait()
            at = self.shard(step, flip)
            self.part[at, :] = self.part[at, :] + self.relay[k]
            self.sent.append(self.send(step, flip, 3 * k))

    def total(self):
        for copy in self.sent:
            copy.wait()
        got = self.got
        own = self.part[self.shard(0, False), :]
        return ((own + got[0]) + (got[1] + got[2])) + (got[3] + got[4])


class Gather:
    def __init__(self, copies, whole, start, ring, half, device):
        self.copies, self.whole, self.start = copies, whole, start
        self.ring, self.half, self.device = ring, half, device

    def send(self, at, step, flip):
        return self.copies.to(self.whole.at[at, :], self.whole.at[at, :], self.device(step, flip))

    def own(self):
        return shard_at(self.start, self.ring, self.half)

    def forward(self, below, above):
        at = shard_at(self.start, lax.rem(self.ring + 3, 4), self.half)
        below.wait_recv()
        up = self.send(at, 1, False)
        at = shard_at(self.start, lax.rem(self.ring + 1, 4), 1 - self.half)
        above.wait_recv()
        self.last = [up, self.send(at, 3, False)]

    def first(self):
        ways = ((1, False), (3, True), (1, True), (3, False), (0, True))
        self.sent = [self.send(self.own(), *way) for way in ways]

    def second(self):
        self.forward(self.sent[0], self.sent[1])

    def finish(self):
        for copy in self.last:
            copy.wait()
        for k, copy in enumerate(self.sent):
            if k < 2:
                copy.wait_send()
            else:
                copy.wait()


class GatherByAxis(Gather):
    def pair(self):
        self.across = self.send(self.own(), 0, True)

    def first(self):
        self.across.wait()
        at = pl.ds(pl.multiple_of(self.start + self.ring * QUARTER, 8), QUARTER)
        self.sent = [self.send(at, 1, False), self.send(at, 3, False)]

    def swap(self, core_peer):
        for copy in self.last:
            copy.wait()
        for copy in self.sent:
            copy.wait_send()
        at = pl.ds(self.start, WIDTH)
        self.half_sent = self.copies.to(self.whole.at[at, :], self.whole.at[at, :], core_peer)

    def finish(self):
        self.half_sent.wait()


class AllSums:
    def __init__(self, tile_out, tile_in, send, receive, place):
        self.tile_out, self.tile_in, self.copies = tile_out, tile_in, Copies(send, receive)
        self.near, self.far = place["near"], place["far"]

    def first(self, lines):
        self.tile_out[0] = jnp.zeros((8, 128), F32)
        for k, line in enumerate(lines):
            self.tile_out[0, pl.ds(k, 1), :] = line
        self.send(0, self.near)

    def send(self, step, peers):
        self.sent = []
        for peer in peers:
            k = self.copies.used
            self.sent.append(self.copies.to(self.tile_out.at[step], self.tile_in.at[k], peer))

    def added(self, step):
        for copy in self.sent:
            copy.wait()
        total = self.tile_out[step]
        for k in range(self.copies.used - len(self.sent), self.copies.used):
            total = total + self.tile_in[k]
        return total

    def second(self):
        self.tile_out[1] = self.added(0)
        self.send(1, self.far)

    def total(self):
        return self.added(1)


def lines_of(value):
    return [value[:, k * 128:(k + 1) * 128] for k in range(value.shape[1] // 128)]


def value_of(tile, first, count):
    return jnp.concatenate([tile[k:k + 1, :] for k in range(first, first + count)], axis=1)


def find_place():
    row, col = lax.axis_index("row"), lax.axis_index("col")
    x_low, z = lax.div(row, 4), lax.rem(row, 4)
    x_high, y, core = lax.div(col, 8), lax.rem(lax.div(col, 2), 4), lax.rem(col, 2)
    place = dict(x_low=x_low, z=z, x_high=x_high, y=y, core=core)

    def device(dz=0, dy=0, low=0, high=0, dcore=0):
        at_z, at_y = lax.rem(z + dz, 4), lax.rem(y + dy, 4)
        at_low = 1 - x_low if low else x_low
        at_high = 1 - x_high if high else x_high
        at_core = 1 - core if dcore else core
        return (at_low * 4 + at_z, at_high * 8 + at_y * 2 + at_core)

    place["on_row"] = lambda step, flip: device(dz=step, low=flip)
    place["on_col"] = lambda step, flip: device(dy=step, high=flip)
    place["core_peer"] = device(dcore=1)
    place["near"] = [
        device(low=a, high=b, dcore=c) for a in (0, 1) for b in (0, 1) for c in (0, 1) if a + b + c
    ]
    place["far"] = [device(dz=a, dy=b) for a in range(4) for b in range(4) if a + b]
    place["other"] = [device(dz=d, low=1) for d in (1, 3)] + [device(dy=d, high=1) for d in (1, 3)]
    place["twin"] = (x_high * 4 + y, x_low * 8 + z * 2 + core)
    place["alone"] = jnp.logical_and(x_low == x_high, z == y)
    return place


def kernel(
    h_hbm, b_hbm, mask_hbm, damping_ref, out_hbm,
    h_stage, h_high, h_low, mask, r0, w0_rows, r2_rows, cols1, cols2,
    part0, part1, relay0, got0, relay1, got1, got_core,
    r0_own, mask_own, mask_sent,
    v_high, v_low, tile_out, tile_in, stage_sem, in_sem, out_sem, send_sem, receive_sem,
    sums_send, sums_receive,
):
    groups, _, width = r0.shape
    place = find_place()
    z, y, core, x_low, x_high = (place[k] for k in ("z", "y", "core", "x_low", "x_high"))
    core_peer = place["core_peer"]
    damping = damping_ref[0]

    def load(k, slot):
        return pltpu.make_async_copy(
            h_hbm.at[pl.ds(k * DEPTH, DEPTH), :], h_stage.at[slot], stage_sem.at[slot]
        )

    loads = []
    for g in range(groups):
        columns = pl.ds(g * width, width)
        loads.append(
            (
                pltpu.make_async_copy(b_hbm.at[:, columns], r0.at[g], in_sem.at[2 * g]),
                pltpu.make_async_copy(mask_hbm.at[:, columns], mask.at[g], in_sem.at[2 * g + 1]),
            )
        )
    for copy in loads[0]:
        copy.start()
    load(0, 0).start()
    load(1, 1).start()
    for copy in loads[1]:
        copy.start()

    barrier = pltpu.get_barrier_semaphore()
    peers = [*place["near"], *place["far"], *place["other"]]
    for peer in peers:
        pl.semaphore_signal(barrier, inc=1, device_id=peer, device_id_type=MESH)

    @pl.when(jnp.logical_not(place["alone"]))
    def _():
        pl.semaphore_signal(barrier, inc=1, device_id=place["twin"], device_id_type=MESH)

    mine, others = pl.multiple_of(core * WIDTH, 8), pl.multiple_of((1 - core) * WIDTH, 8)
    row_own, col_own = shard_at(mine, y, x_high), shard_at(0, z, x_low)
    twin_row, twin_col = shard_at(mine, z, x_low), shard_at(0, y, x_high)

    def first_rows(g):
        for copy in loads[g]:
            copy.wait()

        @pl.loop(0, 8)
        def _(k):
            at = pl.ds(pl.multiple_of(k * QUARTER, 8), QUARTER)
            r0[g, at, :] = r0[g, at, :] * mask[g, at, :].astype(F32)

        mask_sent[g] = mask[g, row_own, :].astype(F32)

    def multiply_first(g, fresh):
        part0[g] = jnp.zeros_like(part0[g])

        @pl.loop(0, DEPTHS)
        def _(k):
            at = pl.ds(pl.multiple_of(k * DEPTH, DEPTH), DEPTH)
            if fresh:
                slot = lax.rem(k, 2)
                load(k, slot).wait()
                high, low = halves(h_stage[slot])
                h_high[at, :] = high
                h_low[at, :] = low

                @pl.when(k < DEPTHS - 2)
                def _():
                    load(k + 2, slot).start()
            b_high, b_low = halves(r0[g, at, :])
            part0[g] += dot3(h_high[at, :], h_low[at, :], b_high, b_low, (0,))

    def split_columns(source, g):
        @pl.loop(0, 4)
        def _(k):
            at = pl.ds(pl.multiple_of(k * QUARTER, 16), QUARTER)
            high, low = halves(source[g, at, :])
            v_high[g, at, :] = high
            v_low[g, at, :] = low

    def multiply_rows(at, g):
        return dot3(h_high[at, :], h_low[at, :], v_high[g], v_low[g], (1,))

    def multiply_block(g, half, k):
        at = pl.ds(pl.multiple_of(half + k * BLOCK, 16), BLOCK)
        part1[g, at, :] = multiply_rows(at, g)

    both = range(groups)
    copies = [Copies(send_sem.at[g], receive_sem.at[g]) for g in both]
    reduce_row = [
        Reduce(copies[g], part0.at[g], relay0.at[g], got0.at[g], 0, z, x_low, place["on_row"]) for g in both
    ]
    reduce_col = [
        Reduce(copies[g], part1.at[g], relay1.at[g], got1.at[g], mine, y, x_high, place["on_col"]) for g in both
    ]
    gather_w0 = [Gather(copies[g], cols1.at[g], 0, z, x_low, place["on_row"]) for g in both]
    gather_r2 = [Gather(copies[g], cols2.at[g], 0, z, x_low, place["on_row"]) for g in both]
    rows_w0 = [GatherByAxis(copies[g], w0_rows.at[g], mine, y, x_high, place["on_col"]) for g in both]
    rows_r2 = [GatherByAxis(copies[g], r2_rows.at[g], mine, y, x_high, place["on_col"]) for g in both]
    sums = [
        AllSums(tile_out.at[s], tile_in.at[s], sums_send.at[s], sums_receive.at[s], place) for s in range(SUMS)
    ]
    lines = width // 128
    moved, w0_moved, r2_moved, swaps, dots0 = {}, {}, {}, {}, {}

    def send_to_twin(g):
        moved[g] = [
            ToTwin(copies[g], r0.at[g, row_own, :], r0_own.at[g], place),
            ToTwin(copies[g], mask_sent.at[g], mask_own.at[g], place),
        ]

    def end_first(g):
        summed = reduce_row[g].total()
        for copy in moved[g]:
            copy.wait()
        r0_here = r0_own[g]
        w0 = mask_own[g] * (summed + damping * r0_here)
        cols1[g, col_own, :] = w0
        gather_w0[g].first()
        w0_moved[g] = ToTwin(copies[g], cols1.at[g, col_own, :], w0_rows.at[g, twin_row, :], place)
        dots0[g] = (column_sum(r0_here, r0_here), column_sum(r0_here, w0))

    def send_other_half(g):
        swaps[g] = []
        pl.loop(0, 2)(lambda k: multiply_block(g, others, k))
        for k in range(2):
            at = pl.ds(pl.multiple_of(others + k * BLOCK, 16), BLOCK)
            inner = pl.ds(k * BLOCK, BLOCK)
            swaps[g].append(copies[g].to(part1.at[g, at, :], got_core.at[g, inner, :], core_peer))

    def add_other_core(g):
        for copy in swaps[g]:
            copy.wait()

        @pl.loop(0, 4)
        def _(k):
            at = pl.ds(pl.multiple_of(mine + k * QUARTER, 8), QUARTER)
            inner = pl.ds(pl.multiple_of(k * QUARTER, 8), QUARTER)
            part1[g, at, :] = part1[g, at, :] + got_core[g, inner, :]

        reduce_col[g].first()

    def sums_of(s, values):
        sums[s].first([line for value in values for line in lines_of(value)])

    shards = {}

    def end_second(g):
        summed = reduce_col[g].total()
        r0_here, w0 = r0[g, row_own, :], w0_rows[g, row_own, :]
        r1 = r0_here - step0[g] * w0
        w1 = w0 - step0[g] * (mask_sent[g] * (summed + damping * w0))
        r2_rows[g, row_own, :] = w1
        sums_of(1 + g, [column_sum(r1, r1), column_sum(r1, w1), column_sum(r1, w0)])

    def make_r2(g):
        tile = sums[1 + g].total()
        norm1, inner1, cross1 = (value_of(tile, k * lines, lines) for k in range(3))
        ratio0 = norm1 / (norm0[g] + epsilon)
        curve1 = inner1 + ratio0 * (2.0 * cross1 + ratio0 * curve0[g])
        step1 = norm1 / (curve1 + epsilon)
        w0 = w0_rows[g, row_own, :]
        along = r2_rows[g, row_own, :] + ratio0 * w0
        r2 = (r0[g, row_own, :] - step0[g] * w0) - step1 * along
        r2_rows[g, row_own, :] = r2
        r2_moved[g] = ToTwin(copies[g], r2_rows.at[g, row_own, :], cols2.at[g, twin_col, :], place)
        rows_r2[g].pair()
        shards[g] = (norm1, ratio0, curve1, step1, column_sum(r2, r2), column_sum(r2, along))

    def dotted(g, half):
        def one(k, total):
            at = pl.ds(pl.multiple_of(half + k * BLOCK, 16), BLOCK)
            return total + column_sum(r2_rows[g, at, :], multiply_rows(at, g))

        return lax.fori_loop(0, 2, one, jnp.zeros((1, width), F32))

    def finish(g):
        tile = sums[3 + g].total()
        norm2, cross2, inner2 = (value_of(tile, k * lines, lines) for k in range(3))
        norm1, ratio0, curve1, step1, _, _ = shards[g]
        ratio1 = norm2 / (norm1 + epsilon)
        curve2 = (inner2 + damping * norm2) + ratio1 * (2.0 * cross2 + ratio1 * curve1)
        step2 = norm2 / (curve2 + epsilon)
        on_d1 = step1 + step2 * ratio1
        on_r0 = step0[g] + on_d1 * (1.0 + ratio0)
        on_w0 = on_d1 * step0[g]

        @pl.loop(0, 8)
        def _(k):
            at = pl.ds(pl.multiple_of(k * QUARTER, 8), QUARTER)
            r0[g, at, :] = (on_r0 * r0[g, at, :] - on_w0 * w0_rows[g, at, :]) + step2 * r2_rows[g, at, :]

        done = pltpu.make_async_copy(r0.at[g], out_hbm.at[:, pl.ds(g * width, width)], out_sem.at[g])
        done.start()
        return done

    first_rows(0)

    @pl.when(jnp.logical_not(place["alone"]))
    def _():
        pl.semaphore_wait(barrier, len(peers) + 1)

    @pl.when(place["alone"])
    def _():
        pl.semaphore_wait(barrier, len(peers))

    send_to_twin(0)
    multiply_first(0, True)
    reduce_row[0].first()
    first_rows(1)
    send_to_twin(1)
    multiply_first(1, False)
    reduce_row[0].second()
    reduce_row[1].first()
    end_first(0)
    reduce_row[1].second()
    gather_w0[0].second()
    w0_moved[0].wait()
    rows_w0[0].pair()
    end_first(1)
    sums_of(0, [dots0[0][0], dots0[1][0], dots0[0][1], dots0[1][1]])
    rows_w0[0].first()
    gather_w0[0].finish()
    split_columns(cols1, 0)
    send_other_half(0)
    gather_w0[1].second()
    sums[0].second()
    rows_w0[0].forward(*rows_w0[0].sent)
    pl.loop(0, 2)(lambda k: multiply_block(0, mine, k))
    add_other_core(0)
    w0_moved[1].wait()
    rows_w0[1].pair()
    gather_w0[1].finish()
    split_columns(cols1, 1)
    reduce_col[0].second()
    rows_w0[1].first()
    send_other_half(1)
    tile = sums[0].total()
    norm0 = [value_of(tile, g * lines, lines) for g in both]
    curve0 = [value_of(tile, (2 + g) * lines, lines) for g in both]
    step0 = [norm0[g] / (curve0[g] + epsilon) for g in both]
    rows_w0[0].swap(core_peer)
    pl.loop(0, 2)(lambda k: multiply_block(1, mine, k))
    add_other_core(1)
    rows_w0[1].forward(*rows_w0[1].sent)
    end_second(0)
    reduce_col[1].second()
    sums[1].second()
    end_second(1)
    make_r2(0)
    sums[2].second()
    r2_moved[0].wait()
    gather_r2[0].first()
    rows_r2[0].first()
    make_r2(1)
    gather_r2[0].second()
    rows_r2[0].forward(*rows_r2[0].sent)
    rows_w0[1].swap(core_peer)
    r2_moved[1].wait()
    gather_r2[1].first()
    rows_r2[1].first()
    gather_r2[0].finish()
    rows_r2[0].swap(core_peer)
    split_columns(cols2, 0)
    inner2 = dotted(0, mine)
    gather_r2[1].second()
    rows_r2[1].forward(*rows_r2[1].sent)
    rows_r2[0].finish()
    sums_of(3, [*shards[0][4:], inner2 + dotted(0, others)])
    gather_r2[1].finish()
    rows_r2[1].swap(core_peer)
    split_columns(cols2, 1)
    sums[3].second()
    inner2 = dotted(1, mine)
    rows_r2[1].finish()
    sums_of(4, [*shards[1][4:], inner2 + dotted(1, others)])
    rows_w0[0].finish()
    rows_w0[1].finish()
    last = [finish(0)]
    sums[4].second()
    last.append(finish(1))
    for copy in last:
        copy.wait()


def on_device(hessian, right_side, mask, damping):
    rows, columns = right_side.shape
    n, width = GROUPS, columns // GROUPS

    def many(*shape, dtype=F32):
        return pltpu.VMEM((n, *shape, width), dtype)

    anywhere = pl.BlockSpec(memory_space=pl.ANY)
    return pl.pallas_call(
        kernel,
        out_shape=jax.ShapeDtypeStruct((rows, columns), F32),
        in_specs=[anywhere] * 3 + [pl.BlockSpec(memory_space=pltpu.SMEM)],
        out_specs=anywhere,
        scratch_shapes=[
            pltpu.VMEM((2, DEPTH, WIDTH), F32),
            pltpu.VMEM((ROWS, WIDTH), BF16),
            pltpu.VMEM((ROWS, WIDTH), BF16),
            many(ROWS, dtype=jnp.int32),
            many(ROWS), many(ROWS), many(ROWS), many(WIDTH), many(WIDTH),
            many(WIDTH), many(ROWS),
            many(2, SHARD), many(5, SHARD), many(2, SHARD), many(5, SHARD), many(WIDTH),
            many(SHARD), many(SHARD), many(SHARD),
            many(WIDTH, dtype=BF16), many(WIDTH, dtype=BF16),
            pltpu.VMEM((SUMS, 2, 8, 128), F32),
            pltpu.VMEM((SUMS, NEAR + FAR, 8, 128), F32),
            pltpu.SemaphoreType.DMA((2,)),
            pltpu.SemaphoreType.DMA((2 * n,)),
            pltpu.SemaphoreType.DMA((n,)),
            pltpu.SemaphoreType.DMA((n, COPIES)),
            pltpu.SemaphoreType.DMA((n, COPIES)),
            pltpu.SemaphoreType.DMA((SUMS, NEAR + FAR)),
            pltpu.SemaphoreType.DMA((SUMS, NEAR + FAR)),
        ],
        compiler_params=pltpu.CompilerParams(
            collective_id=0, has_side_effects=True, vmem_limit_bytes=63 << 20
        ),
    )(hessian, right_side, mask, damping)


def solution(mesh):
    in_specs = (P("row", "col"), P("row", None), P("row", None), P())
    return jax.shard_map(
        on_device, mesh=mesh, in_specs=in_specs, out_specs=P("row", None), check_vma=False
    )
```

```python
import jax
import jax.numpy as jnp
from jax import lax
from jax.experimental import pallas as pl
from jax.experimental.pallas import tpu as pltpu
from jax.sharding import PartitionSpec as P

MESH = pl.DeviceIdType.MESH
F32 = jnp.float32
BF16 = jnp.bfloat16

epsilon = 1e-06

SHARD = 144
QUARTER = 2 * SHARD
WIDTH = 8 * SHARD
ROWS = 16 * SHARD
BLOCK = 4 * SHARD
DEPTH = 256
DEPTHS = ROWS // DEPTH
GROUPS = 2
COPIES = 48
SUMS = 5
NEAR = 7
FAR = 15


def halves(value):
    high = value.astype(BF16)
    return high, (value - high.astype(F32)).astype(BF16)


def dot3(a_high, a_low, b_high, b_low, contract):
    dims = ((contract, (0,)), ((), ()))

    def one(a, b):
        return lax.dot_general(a, b, dims, preferred_element_type=F32)

    return one(a_high, b_high) + (one(a_high, b_low) + one(a_low, b_high))


def column_sum(a, b):
    return jnp.sum(a * b, axis=0, keepdims=True)


class Copies:
    def __init__(self, send, receive):
        self.send, self.receive, self.used = send, receive, 0

    def to(self, source, target, device):
        k = self.used
        self.used += 1
        copy = pltpu.make_async_remote_copy(
            src_ref=source,
            dst_ref=target,
            send_sem=self.send.at[k],
            recv_sem=self.receive.at[k],
            device_id=device,
            device_id_type=MESH,
        )
        copy.start()
        return copy


class ToTwin:
    def __init__(self, copies, source, target, place):
        k = copies.used
        copies.used += 1
        self.alone = place["alone"]
        self.remote = pltpu.make_async_remote_copy(
            src_ref=source,
            dst_ref=target,
            send_sem=copies.send.at[k],
            recv_sem=copies.receive.at[k],
            device_id=place["twin"],
            device_id_type=MESH,
        )
        self.local = pltpu.make_async_copy(source, target, copies.receive.at[k])

        @pl.when(self.alone)
        def _():
            self.local.start()

        @pl.when(jnp.logical_not(self.alone))
        def _():
            self.remote.start()

    def wait(self):
        @pl.when(self.alone)
        def _():
            self.local.wait()

        @pl.when(jnp.logical_not(self.alone))
        def _():
            self.remote.wait()


def shard_at(start, ring, half):
    return pl.ds(pl.multiple_of(start + ring * QUARTER + half * SHARD, 8), SHARD)


class Reduce:
    def __init__(self, copies, part, relay, got, start, ring, half, device):
        self.copies, self.part, self.relay, self.got = copies, part, relay, got
        self.start, self.ring, self.half, self.device = start, ring, half, device

    def shard(self, step, flip):
        half = 1 - self.half if flip else self.half
        return shard_at(self.start, lax.rem(self.ring + step, 4), half)

    def send(self, step, flip, slot):
        at = self.shard(step, flip)
        return self.copies.to(self.part.at[at, :], self.got.at[slot], self.device(step, flip))

    def first(self):
        up = self.copies.to(self.part.at[self.shard(2, False), :], self.relay.at[0], self.device(1, False))
        down = self.copies.to(self.part.at[self.shard(2, True), :], self.relay.at[1], self.device(3, False))
        self.relays = [up, down]
        self.sent = [self.send(1, True, 1), self.send(3, False, 2), self.send(0, True, 4)]

    def second(self):
        for k, (step, flip) in enumerate(((1, False), (3, True))):
            self.relays[k].wait()
            at = self.shard(step, flip)
            self.part[at, :] = self.part[at, :] + self.relay[k]
            self.sent.append(self.send(step, flip, 3 * k))

    def total(self):
        for copy in self.sent:
            copy.wait()
        got = self.got
        own = self.part[self.shard(0, False), :]
        return ((own + got[0]) + (got[1] + got[2])) + (got[3] + got[4])


class Gather:
    def __init__(self, copies, whole, start, ring, half, device):
        self.copies, self.whole, self.start = copies, whole, start
        self.ring, self.half, self.device = ring, half, device

    def send(self, at, step, flip):
        return self.copies.to(self.whole.at[at, :], self.whole.at[at, :], self.device(step, flip))

    def own(self):
        return shard_at(self.start, self.ring, self.half)

    def forward(self, below, above):
        at = shard_at(self.start, lax.rem(self.ring + 3, 4), self.half)
        below.wait_recv()
        up = self.send(at, 1, False)
        at = shard_at(self.start, lax.rem(self.ring + 1, 4), 1 - self.half)
        above.wait_recv()
        self.last = [up, self.send(at, 3, False)]

    def first(self):
        ways = ((1, False), (3, True), (1, True), (3, False), (0, True))
        self.sent = [self.send(self.own(), *way) for way in ways]

    def second(self):
        self.forward(self.sent[0], self.sent[1])

    def finish(self):
        for copy in self.last:
            copy.wait()
        for k, copy in enumerate(self.sent):
            if k < 2:
                copy.wait_send()
            else:
                copy.wait()


class GatherByAxis(Gather):
    def pair(self):
        self.across = self.send(self.own(), 0, True)

    def first(self):
        self.across.wait()
        at = pl.ds(pl.multiple_of(self.start + self.ring * QUARTER, 8), QUARTER)
        self.sent = [self.send(at, 1, False), self.send(at, 3, False)]

    def swap(self, core_peer):
        for copy in self.last:
            copy.wait()
        for copy in self.sent:
            copy.wait_send()
        at = pl.ds(self.start, WIDTH)
        self.half_sent = self.copies.to(self.whole.at[at, :], self.whole.at[at, :], core_peer)

    def finish(self):
        self.half_sent.wait()


class AllSums:
    def __init__(self, tile_out, tile_in, send, receive, place):
        self.tile_out, self.tile_in, self.copies = tile_out, tile_in, Copies(send, receive)
        self.near, self.far = place["near"], place["far"]

    def first(self, lines):
        self.tile_out[0] = jnp.zeros((8, 128), F32)
        for k, line in enumerate(lines):
            self.tile_out[0, pl.ds(k, 1), :] = line
        self.send(0, self.near)

    def send(self, step, peers):
        self.sent = []
        for peer in peers:
            k = self.copies.used
            self.sent.append(self.copies.to(self.tile_out.at[step], self.tile_in.at[k], peer))

    def added(self, step):
        for copy in self.sent:
            copy.wait()
        total = self.tile_out[step]
        for k in range(self.copies.used - len(self.sent), self.copies.used):
            total = total + self.tile_in[k]
        return total

    def second(self):
        self.tile_out[1] = self.added(0)
        self.send(1, self.far)

    def total(self):
        return self.added(1)


def lines_of(value):
    return [value[:, k * 128:(k + 1) * 128] for k in range(value.shape[1] // 128)]


def value_of(tile, first, count):
    return jnp.concatenate([tile[k:k + 1, :] for k in range(first, first + count)], axis=1)


def find_place():
    row, col = lax.axis_index("row"), lax.axis_index("col")
    x_low, z = lax.div(row, 4), lax.rem(row, 4)
    x_high, y, core = lax.div(col, 8), lax.rem(lax.div(col, 2), 4), lax.rem(col, 2)
    place = dict(x_low=x_low, z=z, x_high=x_high, y=y, core=core)

    def device(dz=0, dy=0, low=0, high=0, dcore=0):
        at_z, at_y = lax.rem(z + dz, 4), lax.rem(y + dy, 4)
        at_low = 1 - x_low if low else x_low
        at_high = 1 - x_high if high else x_high
        at_core = 1 - core if dcore else core
        return (at_low * 4 + at_z, at_high * 8 + at_y * 2 + at_core)

    place["on_row"] = lambda step, flip: device(dz=step, low=flip)
    place["on_col"] = lambda step, flip: device(dy=step, high=flip)
    place["core_peer"] = device(dcore=1)
    place["near"] = [
        device(low=a, high=b, dcore=c) for a in (0, 1) for b in (0, 1) for c in (0, 1) if a + b + c
    ]
    place["far"] = [device(dz=a, dy=b) for a in range(4) for b in range(4) if a + b]
    place["other"] = [device(dz=d, low=1) for d in (1, 3)] + [device(dy=d, high=1) for d in (1, 3)]
    place["twin"] = (x_high * 4 + y, x_low * 8 + z * 2 + core)
    place["alone"] = jnp.logical_and(x_low == x_high, z == y)
    return place


def kernel(
    h_hbm, b_hbm, mask_hbm, damping_ref, out_hbm,
    h_stage, h_high, h_low, mask, r0, w0_rows, r2_rows, cols1, cols2,
    part0, part1, relay0, got0, relay1, got1, got_core,
    b_own, mask_own, mask_sent,
    v_high, v_low, tile_out, tile_in, stage_sem, in_sem, out_sem, send_sem, receive_sem,
    sums_send, sums_receive,
):
    groups, _, width = r0.shape
    place = find_place()
    z, y, core, x_low, x_high = (place[k] for k in ("z", "y", "core", "x_low", "x_high"))
    core_peer = place["core_peer"]
    damping = damping_ref[0]

    def load(k, slot):
        return pltpu.make_async_copy(
            h_hbm.at[pl.ds(k * DEPTH, DEPTH), :], h_stage.at[slot], stage_sem.at[slot]
        )

    loads = []
    for g in range(groups):
        columns = pl.ds(g * width, width)
        loads.append(
            (
                pltpu.make_async_copy(b_hbm.at[:, columns], r0.at[g], in_sem.at[2 * g]),
                pltpu.make_async_copy(mask_hbm.at[:, columns], mask.at[g], in_sem.at[2 * g + 1]),
            )
        )
    for copy in loads[0]:
        copy.start()
    load(0, 0).start()
    load(1, 1).start()
    for copy in loads[1]:
        copy.start()

    barrier = pltpu.get_barrier_semaphore()
    peers = [*place["near"], *place["far"], *place["other"]]
    for peer in peers:
        pl.semaphore_signal(barrier, inc=1, device_id=peer, device_id_type=MESH)

    @pl.when(jnp.logical_not(place["alone"]))
    def _():
        pl.semaphore_signal(barrier, inc=1, device_id=place["twin"], device_id_type=MESH)

    mine, others = pl.multiple_of(core * WIDTH, 8), pl.multiple_of((1 - core) * WIDTH, 8)
    row_own, col_own = shard_at(mine, y, x_high), shard_at(0, z, x_low)
    twin_row, twin_col = shard_at(mine, z, x_low), shard_at(0, y, x_high)

    def first_rows(g):
        for copy in loads[g]:
            copy.wait()

        @pl.loop(0, 8)
        def _(k):
            at = pl.ds(pl.multiple_of(k * QUARTER, 8), QUARTER)
            r0[g, at, :] = r0[g, at, :] * mask[g, at, :].astype(F32)

        mask_sent[g] = mask[g, row_own, :].astype(F32)

    def multiply_first(g, fresh):
        part0[g] = jnp.zeros_like(part0[g])

        @pl.loop(0, DEPTHS)
        def _(k):
            at = pl.ds(pl.multiple_of(k * DEPTH, DEPTH), DEPTH)
            if fresh:
                slot = lax.rem(k, 2)
                load(k, slot).wait()
                high, low = halves(h_stage[slot])
                h_high[at, :] = high
                h_low[at, :] = low

                @pl.when(k < DEPTHS - 2)
                def _():
                    load(k + 2, slot).start()
            b_high, b_low = halves(r0[g, at, :])
            part0[g] += dot3(h_high[at, :], h_low[at, :], b_high, b_low, (0,))

    def split_columns(source, g):
        @pl.loop(0, 4)
        def _(k):
            at = pl.ds(pl.multiple_of(k * QUARTER, 16), QUARTER)
            high, low = halves(source[g, at, :])
            v_high[g, at, :] = high
            v_low[g, at, :] = low

    def multiply_rows(at, g):
        return dot3(h_high[at, :], h_low[at, :], v_high[g], v_low[g], (1,))

    def multiply_block(g, half, k):
        at = pl.ds(pl.multiple_of(half + k * BLOCK, 16), BLOCK)
        part1[g, at, :] = multiply_rows(at, g)

    both = range(groups)
    copies = [Copies(send_sem.at[g], receive_sem.at[g]) for g in both]
    reduce_row = [
        Reduce(copies[g], part0.at[g], relay0.at[g], got0.at[g], 0, z, x_low, place["on_row"]) for g in both
    ]
    reduce_col = [
        Reduce(copies[g], part1.at[g], relay1.at[g], got1.at[g], mine, y, x_high, place["on_col"]) for g in both
    ]
    gather_w0 = [Gather(copies[g], cols1.at[g], 0, z, x_low, place["on_row"]) for g in both]
    gather_r2 = [Gather(copies[g], cols2.at[g], 0, z, x_low, place["on_row"]) for g in both]
    rows_w0 = [GatherByAxis(copies[g], w0_rows.at[g], mine, y, x_high, place["on_col"]) for g in both]
    rows_r2 = [GatherByAxis(copies[g], r2_rows.at[g], mine, y, x_high, place["on_col"]) for g in both]
    sums = [
        AllSums(tile_out.at[s], tile_in.at[s], sums_send.at[s], sums_receive.at[s], place) for s in range(SUMS)
    ]
    lines = width // 128
    w0_moved, r2_moved, swaps, dots0 = {}, {}, {}, {}

    def end_first(g):
        summed = reduce_row[g].total()
        if g == 0:
            for copy in moved:
                copy.wait()
        columns = pl.ds(g * width, width)
        keep = mask_own[:, columns].astype(F32)
        r0_here = keep * b_own[:, columns]
        w0 = keep * (summed + damping * r0_here)
        cols1[g, col_own, :] = w0
        gather_w0[g].first()
        w0_moved[g] = ToTwin(copies[g], cols1.at[g, col_own, :], w0_rows.at[g, twin_row, :], place)
        dots0[g] = (column_sum(r0_here, r0_here), column_sum(r0_here, w0))

    def send_other_half(g):
        swaps[g] = []
        pl.loop(0, 2)(lambda k: multiply_block(g, others, k))
        for k in range(2):
            at = pl.ds(pl.multiple_of(others + k * BLOCK, 16), BLOCK)
            inner = pl.ds(k * BLOCK, BLOCK)
            swaps[g].append(copies[g].to(part1.at[g, at, :], got_core.at[g, inner, :], core_peer))

    def add_other_core(g):
        for copy in swaps[g]:
            copy.wait()

        @pl.loop(0, 4)
        def _(k):
            at = pl.ds(pl.multiple_of(mine + k * QUARTER, 8), QUARTER)
            inner = pl.ds(pl.multiple_of(k * QUARTER, 8), QUARTER)
            part1[g, at, :] = part1[g, at, :] + got_core[g, inner, :]

        reduce_col[g].first()

    def sums_of(s, values):
        sums[s].first([line for value in values for line in lines_of(value)])

    shards = {}

    def end_second(g):
        summed = reduce_col[g].total()
        r0_here, w0 = r0[g, row_own, :], w0_rows[g, row_own, :]
        r1 = r0_here - step0[g] * w0
        w1 = w0 - step0[g] * (mask_sent[g] * (summed + damping * w0))
        r2_rows[g, row_own, :] = w1
        sums_of(1 + g, [column_sum(r1, r1), column_sum(r1, w1), column_sum(r1, w0)])

    def make_r2(g):
        tile = sums[1 + g].total()
        norm1, inner1, cross1 = (value_of(tile, k * lines, lines) for k in range(3))
        ratio0 = norm1 / (norm0[g] + epsilon)
        curve1 = inner1 + ratio0 * (2.0 * cross1 + ratio0 * curve0[g])
        step1 = norm1 / (curve1 + epsilon)
        w0 = w0_rows[g, row_own, :]
        along = r2_rows[g, row_own, :] + ratio0 * w0
        r2 = (r0[g, row_own, :] - step0[g] * w0) - step1 * along
        r2_rows[g, row_own, :] = r2
        r2_moved[g] = ToTwin(copies[g], r2_rows.at[g, row_own, :], cols2.at[g, twin_col, :], place)
        rows_r2[g].pair()
        shards[g] = (norm1, ratio0, curve1, step1, column_sum(r2, r2), column_sum(r2, along))

    def dotted(g, half):
        def one(k, total):
            at = pl.ds(pl.multiple_of(half + k * BLOCK, 16), BLOCK)
            return total + column_sum(r2_rows[g, at, :], multiply_rows(at, g))

        return lax.fori_loop(0, 2, one, jnp.zeros((1, width), F32))

    def finish(g):
        tile = sums[3 + g].total()
        norm2, cross2, inner2 = (value_of(tile, k * lines, lines) for k in range(3))
        norm1, ratio0, curve1, step1, _, _ = shards[g]
        ratio1 = norm2 / (norm1 + epsilon)
        curve2 = (inner2 + damping * norm2) + ratio1 * (2.0 * cross2 + ratio1 * curve1)
        step2 = norm2 / (curve2 + epsilon)
        on_d1 = step1 + step2 * ratio1
        on_r0 = step0[g] + on_d1 * (1.0 + ratio0)
        on_w0 = on_d1 * step0[g]

        @pl.loop(0, 8)
        def _(k):
            at = pl.ds(pl.multiple_of(k * QUARTER, 8), QUARTER)
            r0[g, at, :] = (on_r0 * r0[g, at, :] - on_w0 * w0_rows[g, at, :]) + step2 * r2_rows[g, at, :]

        done = pltpu.make_async_copy(r0.at[g], out_hbm.at[:, pl.ds(g * width, width)], out_sem.at[g])
        done.start()
        return done

    @pl.when(jnp.logical_not(place["alone"]))
    def _():
        pl.semaphore_wait(barrier, len(peers) + 1)

    @pl.when(place["alone"])
    def _():
        pl.semaphore_wait(barrier, len(peers))

    moved = [
        ToTwin(copies[0], b_hbm.at[row_own, :], b_own, place),
        ToTwin(copies[0], mask_hbm.at[row_own, :], mask_own, place),
    ]
    first_rows(0)
    multiply_first(0, True)
    reduce_row[0].first()
    first_rows(1)
    multiply_first(1, False)
    reduce_row[0].second()
    reduce_row[1].first()
    end_first(0)
    reduce_row[1].second()
    gather_w0[0].second()
    w0_moved[0].wait()
    rows_w0[0].pair()
    end_first(1)
    sums_of(0, [dots0[0][0], dots0[1][0], dots0[0][1], dots0[1][1]])
    rows_w0[0].first()
    gather_w0[0].finish()
    split_columns(cols1, 0)
    send_other_half(0)
    gather_w0[1].second()
    sums[0].second()
    rows_w0[0].forward(*rows_w0[0].sent)
    pl.loop(0, 2)(lambda k: multiply_block(0, mine, k))
    add_other_core(0)
    w0_moved[1].wait()
    rows_w0[1].pair()
    gather_w0[1].finish()
    split_columns(cols1, 1)
    reduce_col[0].second()
    rows_w0[1].first()
    send_other_half(1)
    tile = sums[0].total()
    norm0 = [value_of(tile, g * lines, lines) for g in both]
    curve0 = [value_of(tile, (2 + g) * lines, lines) for g in both]
    step0 = [norm0[g] / (curve0[g] + epsilon) for g in both]
    rows_w0[0].swap(core_peer)
    pl.loop(0, 2)(lambda k: multiply_block(1, mine, k))
    add_other_core(1)
    rows_w0[1].forward(*rows_w0[1].sent)
    end_second(0)
    reduce_col[1].second()
    sums[1].second()
    end_second(1)
    make_r2(0)
    sums[2].second()
    r2_moved[0].wait()
    gather_r2[0].first()
    rows_r2[0].first()
    make_r2(1)
    gather_r2[0].second()
    rows_r2[0].forward(*rows_r2[0].sent)
    rows_w0[1].swap(core_peer)
    r2_moved[1].wait()
    gather_r2[1].first()
    rows_r2[1].first()
    gather_r2[0].finish()
    rows_r2[0].swap(core_peer)
    split_columns(cols2, 0)
    inner2 = dotted(0, mine)
    gather_r2[1].second()
    rows_r2[1].forward(*rows_r2[1].sent)
    rows_r2[0].finish()
    sums_of(3, [*shards[0][4:], inner2 + dotted(0, others)])
    gather_r2[1].finish()
    rows_r2[1].swap(core_peer)
    split_columns(cols2, 1)
    sums[3].second()
    inner2 = dotted(1, mine)
    rows_r2[1].finish()
    sums_of(4, [*shards[1][4:], inner2 + dotted(1, others)])
    rows_w0[0].finish()
    rows_w0[1].finish()
    last = [finish(0)]
    sums[4].second()
    last.append(finish(1))
    for copy in last:
        copy.wait()


def on_device(hessian, right_side, mask, damping):
    rows, columns = right_side.shape
    n, width = GROUPS, columns // GROUPS

    def many(*shape, dtype=F32):
        return pltpu.VMEM((n, *shape, width), dtype)

    anywhere = pl.BlockSpec(memory_space=pl.ANY)
    return pl.pallas_call(
        kernel,
        out_shape=jax.ShapeDtypeStruct((rows, columns), F32),
        in_specs=[anywhere] * 3 + [pl.BlockSpec(memory_space=pltpu.SMEM)],
        out_specs=anywhere,
        scratch_shapes=[
            pltpu.VMEM((2, DEPTH, WIDTH), F32),
            pltpu.VMEM((ROWS, WIDTH), BF16),
            pltpu.VMEM((ROWS, WIDTH), BF16),
            many(ROWS, dtype=jnp.int32),
            many(ROWS), many(ROWS), many(ROWS), many(WIDTH), many(WIDTH),
            many(WIDTH), many(ROWS),
            many(2, SHARD), many(5, SHARD), many(2, SHARD), many(5, SHARD), many(WIDTH),
            pltpu.VMEM((SHARD, columns), F32), pltpu.VMEM((SHARD, columns), jnp.int32), many(SHARD),
            many(WIDTH, dtype=BF16), many(WIDTH, dtype=BF16),
            pltpu.VMEM((SUMS, 2, 8, 128), F32),
            pltpu.VMEM((SUMS, NEAR + FAR, 8, 128), F32),
            pltpu.SemaphoreType.DMA((2,)),
            pltpu.SemaphoreType.DMA((2 * n,)),
            pltpu.SemaphoreType.DMA((n,)),
            pltpu.SemaphoreType.DMA((n, COPIES)),
            pltpu.SemaphoreType.DMA((n, COPIES)),
            pltpu.SemaphoreType.DMA((SUMS, NEAR + FAR)),
            pltpu.SemaphoreType.DMA((SUMS, NEAR + FAR)),
        ],
        compiler_params=pltpu.CompilerParams(
            collective_id=0, has_side_effects=True, vmem_limit_bytes=63 << 20
        ),
    )(hessian, right_side, mask, damping)


def solution(mesh):
    in_specs = (P("row", "col"), P("row", None), P("row", None), P())
    return jax.shard_map(
        on_device, mesh=mesh, in_specs=in_specs, out_specs=P("row", None), check_vma=False
    )
```

```python
import jax
import jax.numpy as jnp
from jax import lax
from jax.experimental import pallas as pl
from jax.experimental.pallas import tpu as pltpu
from jax.sharding import PartitionSpec as P

MESH = pl.DeviceIdType.MESH
F32 = jnp.float32
BF16 = jnp.bfloat16

epsilon = 1e-06

SHARD = 144
QUARTER = 2 * SHARD
WIDTH = 8 * SHARD
ROWS = 16 * SHARD
BLOCK = 4 * SHARD
DEPTH = 256
DEPTHS = ROWS // DEPTH
GROUPS = 2
COPIES = 48
SUMS = 5
NEAR = 7
FAR = 15


def halves(value):
    high = value.astype(BF16)
    return high, (value - high.astype(F32)).astype(BF16)


def dot3(a_high, a_low, b_high, b_low, contract):
    dims = ((contract, (0,)), ((), ()))

    def one(a, b):
        return lax.dot_general(a, b, dims, preferred_element_type=F32)

    return one(a_high, b_high) + (one(a_high, b_low) + one(a_low, b_high))


def column_sum(a, b):
    return jnp.sum(a * b, axis=0, keepdims=True)


class Copies:
    def __init__(self, send, receive):
        self.send, self.receive, self.used = send, receive, 0

    def to(self, source, target, device):
        k = self.used
        self.used += 1
        copy = pltpu.make_async_remote_copy(
            src_ref=source,
            dst_ref=target,
            send_sem=self.send.at[k],
            recv_sem=self.receive.at[k],
            device_id=device,
            device_id_type=MESH,
        )
        copy.start()
        return copy


class ToTwin:
    def __init__(self, copies, source, target, device, alone):
        k = copies.used
        copies.used += 1
        self.alone = alone
        self.remote = pltpu.make_async_remote_copy(
            src_ref=source,
            dst_ref=target,
            send_sem=copies.send.at[k],
            recv_sem=copies.receive.at[k],
            device_id=device,
            device_id_type=MESH,
        )
        self.local = pltpu.make_async_copy(source, target, copies.receive.at[k])

        @pl.when(self.alone)
        def _():
            self.local.start()

        @pl.when(jnp.logical_not(self.alone))
        def _():
            self.remote.start()

    def wait(self):
        @pl.when(self.alone)
        def _():
            self.local.wait()

        @pl.when(jnp.logical_not(self.alone))
        def _():
            self.remote.wait()


def shard_at(start, ring, half):
    return pl.ds(pl.multiple_of(start + ring * QUARTER + half * SHARD, 8), SHARD)


class Reduce:
    def __init__(self, copies, part, relay, got, start, ring, half, device):
        self.copies, self.part, self.relay, self.got = copies, part, relay, got
        self.start, self.ring, self.half, self.device = start, ring, half, device

    def shard(self, step, flip):
        half = 1 - self.half if flip else self.half
        return shard_at(self.start, lax.rem(self.ring + step, 4), half)

    def send(self, step, flip, slot):
        at = self.shard(step, flip)
        return self.copies.to(self.part.at[at, :], self.got.at[slot], self.device(step, flip))

    def first(self):
        up = self.copies.to(self.part.at[self.shard(2, False), :], self.relay.at[0], self.device(1, False))
        down = self.copies.to(self.part.at[self.shard(2, True), :], self.relay.at[1], self.device(3, False))
        self.relays = [up, down]
        self.sent = [self.send(1, True, 1), self.send(3, False, 2), self.send(0, True, 4)]

    def second(self):
        for k, (step, flip) in enumerate(((1, False), (3, True))):
            self.relays[k].wait()
            at = self.shard(step, flip)
            self.part[at, :] = self.part[at, :] + self.relay[k]
            self.sent.append(self.send(step, flip, 3 * k))

    def total(self):
        for copy in self.sent:
            copy.wait()
        got = self.got
        own = self.part[self.shard(0, False), :]
        return ((own + got[0]) + (got[1] + got[2])) + (got[3] + got[4])


class Gather:
    def __init__(self, copies, whole, start, ring, half, device):
        self.copies, self.whole, self.start = copies, whole, start
        self.ring, self.half, self.device = ring, half, device

    def send(self, at, step, flip):
        return self.copies.to(self.whole.at[at, :], self.whole.at[at, :], self.device(step, flip))

    def own(self):
        return shard_at(self.start, self.ring, self.half)

    def forward(self, below, above):
        at = shard_at(self.start, lax.rem(self.ring + 3, 4), self.half)
        below.wait_recv()
        up = self.send(at, 1, False)
        at = shard_at(self.start, lax.rem(self.ring + 1, 4), 1 - self.half)
        above.wait_recv()
        self.last = [up, self.send(at, 3, False)]

    def first(self):
        ways = ((1, False), (3, True), (1, True), (3, False), (0, True))
        self.sent = [self.send(self.own(), *way) for way in ways]

    def second(self):
        self.forward(self.sent[0], self.sent[1])

    def finish(self):
        for copy in self.last:
            copy.wait()
        for k, copy in enumerate(self.sent):
            if k < 2:
                copy.wait_send()
            else:
                copy.wait()


class GatherByAxis(Gather):
    def pair(self):
        self.across = self.send(self.own(), 0, True)

    def first(self):
        self.across.wait()
        at = pl.ds(pl.multiple_of(self.start + self.ring * QUARTER, 8), QUARTER)
        self.sent = [self.send(at, 1, False), self.send(at, 3, False)]

    def swap(self, core_peer):
        for copy in self.last:
            copy.wait()
        for copy in self.sent:
            copy.wait_send()
        at = pl.ds(self.start, WIDTH)
        self.half_sent = self.copies.to(self.whole.at[at, :], self.whole.at[at, :], core_peer)

    def finish(self):
        self.half_sent.wait()


class AllSums:
    def __init__(self, tile_out, tile_in, send, receive, place):
        self.tile_out, self.tile_in, self.copies = tile_out, tile_in, Copies(send, receive)
        self.near, self.far = place["near"], place["far"]

    def first(self, lines):
        self.tile_out[0] = jnp.zeros((8, 128), F32)
        for k, line in enumerate(lines):
            self.tile_out[0, pl.ds(k, 1), :] = line
        self.send(0, self.near)

    def send(self, step, peers):
        self.sent = []
        for peer in peers:
            k = self.copies.used
            self.sent.append(self.copies.to(self.tile_out.at[step], self.tile_in.at[k], peer))

    def added(self, step):
        for copy in self.sent:
            copy.wait()
        total = self.tile_out[step]
        for k in range(self.copies.used - len(self.sent), self.copies.used):
            total = total + self.tile_in[k]
        return total

    def second(self):
        self.tile_out[1] = self.added(0)
        self.send(1, self.far)

    def total(self):
        return self.added(1)


def lines_of(value):
    return [value[:, k * 128:(k + 1) * 128] for k in range(value.shape[1] // 128)]


def value_of(tile, first, count):
    return jnp.concatenate([tile[k:k + 1, :] for k in range(first, first + count)], axis=1)


def find_place():
    row, col = lax.axis_index("row"), lax.axis_index("col")
    x_low, z = lax.div(row, 4), lax.rem(row, 4)
    x_high, y, core = lax.div(col, 8), lax.rem(lax.div(col, 2), 4), lax.rem(col, 2)
    place = dict(x_low=x_low, z=z, x_high=x_high, y=y, core=core)

    def device(dz=0, dy=0, low=0, high=0, dcore=0):
        at_z, at_y = lax.rem(z + dz, 4), lax.rem(y + dy, 4)
        at_low = 1 - x_low if low else x_low
        at_high = 1 - x_high if high else x_high
        at_core = 1 - core if dcore else core
        return (at_low * 4 + at_z, at_high * 8 + at_y * 2 + at_core)

    place["on_row"] = lambda step, flip: device(dz=step, low=flip)
    place["on_col"] = lambda step, flip: device(dy=step, high=flip)
    place["core_peer"] = device(dcore=1)
    place["near"] = [
        device(low=a, high=b, dcore=c) for a in (0, 1) for b in (0, 1) for c in (0, 1) if a + b + c
    ]
    place["far"] = [device(dz=a, dy=b) for a in range(4) for b in range(4) if a + b]
    place["other"] = [device(dz=d, low=1) for d in (1, 3)] + [device(dy=d, high=1) for d in (1, 3)]
    ring, half = lax.rem(z + core, 4), lax.rem(x_low + core, 2)
    place["ring"], place["half"] = ring, half
    to_half = lax.rem(x_high + core, 2)

    def to_columns(turn, flip):
        at_low = 1 - to_half if flip else to_half
        return (at_low * 4 + lax.rem(y + 8 - core - turn, 4), x_low * 8 + z * 2 + core)

    def to_rows(turn, flip):
        at_high = 1 - half if flip else half
        return (x_high * 4 + y, at_high * 8 + lax.rem(ring + turn, 4) * 2 + core)

    place["to_columns"], place["to_rows"] = to_columns(0, False), to_rows(0, False)
    place["mask_to"], place["mask_from"] = to_columns(2, True), to_rows(2, True)
    place["alone"] = jnp.logical_and(jnp.logical_and(x_low == x_high, z == y), core == 0)
    return place


def kernel(
    h_hbm, b_hbm, mask_hbm, damping_ref, out_hbm,
    h_stage, h_high, h_low, mask, r0, w0_rows, r2_rows, cols1, cols2,
    part0, part1, relay0, got0, relay1, got1, got_core,
    b_own, mask_own, mask_sent,
    v_high, v_low, tile_out, tile_in, stage_sem, in_sem, out_sem, send_sem, receive_sem,
    sums_send, sums_receive,
):
    groups, _, width = r0.shape
    place = find_place()
    z, y, core, x_low, x_high = (place[k] for k in ("z", "y", "core", "x_low", "x_high"))
    core_peer = place["core_peer"]
    damping = damping_ref[0]

    def load(k, slot):
        return pltpu.make_async_copy(
            h_hbm.at[pl.ds(k * DEPTH, DEPTH), :], h_stage.at[slot], stage_sem.at[slot]
        )

    loads = []
    for g in range(groups):
        columns = pl.ds(g * width, width)
        loads.append(
            (
                pltpu.make_async_copy(b_hbm.at[:, columns], r0.at[g], in_sem.at[2 * g]),
                pltpu.make_async_copy(mask_hbm.at[:, columns], mask.at[g], in_sem.at[2 * g + 1]),
            )
        )
    for copy in loads[0]:
        copy.start()
    load(0, 0).start()
    load(1, 1).start()
    for copy in loads[1]:
        copy.start()

    barrier = pltpu.get_barrier_semaphore()
    peers = [*place["near"], *place["far"], *place["other"], place["mask_from"]]
    for peer in peers:
        pl.semaphore_signal(barrier, inc=1, device_id=peer, device_id_type=MESH)

    @pl.when(jnp.logical_not(place["alone"]))
    def _():
        for peer in (place["to_rows"], place["to_columns"]):
            pl.semaphore_signal(barrier, inc=1, device_id=peer, device_id_type=MESH)

    mine, others = pl.multiple_of(core * WIDTH, 8), pl.multiple_of((1 - core) * WIDTH, 8)
    ring, half = place["ring"], place["half"]
    row_own, col_own = shard_at(mine, y, x_high), shard_at(0, ring, half)
    twin_row, twin_col = shard_at(mine, ring, half), shard_at(0, y, x_high)
    mask_rows = shard_at(mine, lax.rem(y + 2, 4), 1 - x_high)
    alone = place["alone"]

    def first_rows(g):
        for copy in loads[g]:
            copy.wait()

        @pl.loop(0, 8)
        def _(k):
            at = pl.ds(pl.multiple_of(k * QUARTER, 8), QUARTER)
            r0[g, at, :] = r0[g, at, :] * mask[g, at, :].astype(F32)

        mask_sent[g] = mask[g, row_own, :].astype(F32)

    def multiply_first(g, fresh):
        part0[g] = jnp.zeros_like(part0[g])

        @pl.loop(0, DEPTHS)
        def _(k):
            at = pl.ds(pl.multiple_of(k * DEPTH, DEPTH), DEPTH)
            if fresh:
                slot = lax.rem(k, 2)
                load(k, slot).wait()
                high, low = halves(h_stage[slot])
                h_high[at, :] = high
                h_low[at, :] = low

                @pl.when(k < DEPTHS - 2)
                def _():
                    load(k + 2, slot).start()
            b_high, b_low = halves(r0[g, at, :])
            part0[g] += dot3(h_high[at, :], h_low[at, :], b_high, b_low, (0,))

    def split_columns(source, g):
        @pl.loop(0, 4)
        def _(k):
            at = pl.ds(pl.multiple_of(k * QUARTER, 16), QUARTER)
            high, low = halves(source[g, at, :])
            v_high[g, at, :] = high
            v_low[g, at, :] = low

    def multiply_rows(at, g):
        return dot3(h_high[at, :], h_low[at, :], v_high[g], v_low[g], (1,))

    def multiply_block(g, half, k):
        at = pl.ds(pl.multiple_of(half + k * BLOCK, 16), BLOCK)
        part1[g, at, :] = multiply_rows(at, g)

    both = range(groups)
    copies = [Copies(send_sem.at[g], receive_sem.at[g]) for g in both]
    reduce_row = [
        Reduce(copies[g], part0.at[g], relay0.at[g], got0.at[g], 0, ring, half, place["on_row"]) for g in both
    ]
    reduce_col = [
        Reduce(copies[g], part1.at[g], relay1.at[g], got1.at[g], mine, y, x_high, place["on_col"]) for g in both
    ]
    gather_w0 = [Gather(copies[g], cols1.at[g], 0, ring, half, place["on_row"]) for g in both]
    gather_r2 = [Gather(copies[g], cols2.at[g], 0, ring, half, place["on_row"]) for g in both]
    rows_w0 = [GatherByAxis(copies[g], w0_rows.at[g], mine, y, x_high, place["on_col"]) for g in both]
    rows_r2 = [GatherByAxis(copies[g], r2_rows.at[g], mine, y, x_high, place["on_col"]) for g in both]
    sums = [
        AllSums(tile_out.at[s], tile_in.at[s], sums_send.at[s], sums_receive.at[s], place) for s in range(SUMS)
    ]
    lines = width // 128
    w0_moved, r2_moved, swaps, dots0 = {}, {}, {}, {}

    def end_first(g):
        summed = reduce_row[g].total()
        if g == 0:
            for copy in moved:
                copy.wait()
        columns = pl.ds(g * width, width)
        keep = mask_own[:, columns].astype(F32)
        r0_here = keep * b_own[:, columns]
        w0 = keep * (summed + damping * r0_here)
        cols1[g, col_own, :] = w0
        gather_w0[g].first()
        here, there = cols1.at[g, col_own, :], w0_rows.at[g, twin_row, :]
        w0_moved[g] = ToTwin(copies[g], here, there, place["to_rows"], alone)
        dots0[g] = (column_sum(r0_here, r0_here), column_sum(r0_here, w0))

    def send_other_half(g):
        swaps[g] = []
        pl.loop(0, 2)(lambda k: multiply_block(g, others, k))
        for k in range(2):
            at = pl.ds(pl.multiple_of(others + k * BLOCK, 16), BLOCK)
            inner = pl.ds(k * BLOCK, BLOCK)
            swaps[g].append(copies[g].to(part1.at[g, at, :], got_core.at[g, inner, :], core_peer))

    def add_other_core(g):
        for copy in swaps[g]:
            copy.wait()

        @pl.loop(0, 4)
        def _(k):
            at = pl.ds(pl.multiple_of(mine + k * QUARTER, 8), QUARTER)
            inner = pl.ds(pl.multiple_of(k * QUARTER, 8), QUARTER)
            part1[g, at, :] = part1[g, at, :] + got_core[g, inner, :]

        reduce_col[g].first()

    def sums_of(s, values):
        sums[s].first([line for value in values for line in lines_of(value)])

    shards = {}

    def end_second(g):
        summed = reduce_col[g].total()
        r0_here, w0 = r0[g, row_own, :], w0_rows[g, row_own, :]
        r1 = r0_here - step0[g] * w0
        w1 = w0 - step0[g] * (mask_sent[g] * (summed + damping * w0))
        r2_rows[g, row_own, :] = w1
        sums_of(1 + g, [column_sum(r1, r1), column_sum(r1, w1), column_sum(r1, w0)])

    def make_r2(g):
        tile = sums[1 + g].total()
        norm1, inner1, cross1 = (value_of(tile, k * lines, lines) for k in range(3))
        ratio0 = norm1 / (norm0[g] + epsilon)
        curve1 = inner1 + ratio0 * (2.0 * cross1 + ratio0 * curve0[g])
        step1 = norm1 / (curve1 + epsilon)
        w0 = w0_rows[g, row_own, :]
        along = r2_rows[g, row_own, :] + ratio0 * w0
        r2 = (r0[g, row_own, :] - step0[g] * w0) - step1 * along
        r2_rows[g, row_own, :] = r2
        here, there = r2_rows.at[g, row_own, :], cols2.at[g, twin_col, :]
        r2_moved[g] = ToTwin(copies[g], here, there, place["to_columns"], alone)
        rows_r2[g].pair()
        shards[g] = (norm1, ratio0, curve1, step1, column_sum(r2, r2), column_sum(r2, along))

    def dotted(g, half):
        def one(k, total):
            at = pl.ds(pl.multiple_of(half + k * BLOCK, 16), BLOCK)
            return total + column_sum(r2_rows[g, at, :], multiply_rows(at, g))

        return lax.fori_loop(0, 2, one, jnp.zeros((1, width), F32))

    def finish(g):
        tile = sums[3 + g].total()
        norm2, cross2, inner2 = (value_of(tile, k * lines, lines) for k in range(3))
        norm1, ratio0, curve1, step1, _, _ = shards[g]
        ratio1 = norm2 / (norm1 + epsilon)
        curve2 = (inner2 + damping * norm2) + ratio1 * (2.0 * cross2 + ratio1 * curve1)
        step2 = norm2 / (curve2 + epsilon)
        on_d1 = step1 + step2 * ratio1
        on_r0 = step0[g] + on_d1 * (1.0 + ratio0)
        on_w0 = on_d1 * step0[g]

        @pl.loop(0, 8)
        def _(k):
            at = pl.ds(pl.multiple_of(k * QUARTER, 8), QUARTER)
            r0[g, at, :] = (on_r0 * r0[g, at, :] - on_w0 * w0_rows[g, at, :]) + step2 * r2_rows[g, at, :]

        done = pltpu.make_async_copy(r0.at[g], out_hbm.at[:, pl.ds(g * width, width)], out_sem.at[g])
        done.start()
        return done

    @pl.when(jnp.logical_not(place["alone"]))
    def _():
        pl.semaphore_wait(barrier, len(peers) + 2)

    @pl.when(place["alone"])
    def _():
        pl.semaphore_wait(barrier, len(peers))

    moved = [
        ToTwin(copies[0], b_hbm.at[row_own, :], b_own, place["to_columns"], alone),
        copies[0].to(mask_hbm.at[mask_rows, :], mask_own, place["mask_to"]),
    ]
    first_rows(0)
    multiply_first(0, True)
    reduce_row[0].first()
    first_rows(1)
    multiply_first(1, False)
    reduce_row[0].second()
    reduce_row[1].first()
    end_first(0)
    reduce_row[1].second()
    gather_w0[0].second()
    w0_moved[0].wait()
    rows_w0[0].pair()
    end_first(1)
    sums_of(0, [dots0[0][0], dots0[1][0], dots0[0][1], dots0[1][1]])
    rows_w0[0].first()
    gather_w0[0].finish()
    split_columns(cols1, 0)
    send_other_half(0)
    gather_w0[1].second()
    sums[0].second()
    rows_w0[0].forward(*rows_w0[0].sent)
    pl.loop(0, 2)(lambda k: multiply_block(0, mine, k))
    add_other_core(0)
    w0_moved[1].wait()
    rows_w0[1].pair()
    gather_w0[1].finish()
    split_columns(cols1, 1)
    reduce_col[0].second()
    rows_w0[1].first()
    send_other_half(1)
    tile = sums[0].total()
    norm0 = [value_of(tile, g * lines, lines) for g in both]
    curve0 = [value_of(tile, (2 + g) * lines, lines) for g in both]
    step0 = [norm0[g] / (curve0[g] + epsilon) for g in both]
    rows_w0[0].swap(core_peer)
    pl.loop(0, 2)(lambda k: multiply_block(1, mine, k))
    add_other_core(1)
    rows_w0[1].forward(*rows_w0[1].sent)
    end_second(0)
    reduce_col[1].second()
    sums[1].second()
    end_second(1)
    make_r2(0)
    sums[2].second()
    r2_moved[0].wait()
    gather_r2[0].first()
    rows_r2[0].first()
    make_r2(1)
    gather_r2[0].second()
    rows_r2[0].forward(*rows_r2[0].sent)
    rows_w0[1].swap(core_peer)
    r2_moved[1].wait()
    gather_r2[1].first()
    rows_r2[1].first()
    gather_r2[0].finish()
    rows_r2[0].swap(core_peer)
    split_columns(cols2, 0)
    inner2 = dotted(0, mine)
    gather_r2[1].second()
    rows_r2[1].forward(*rows_r2[1].sent)
    rows_r2[0].finish()
    sums_of(3, [*shards[0][4:], inner2 + dotted(0, others)])
    gather_r2[1].finish()
    rows_r2[1].swap(core_peer)
    split_columns(cols2, 1)
    sums[3].second()
    inner2 = dotted(1, mine)
    rows_r2[1].finish()
    sums_of(4, [*shards[1][4:], inner2 + dotted(1, others)])
    rows_w0[0].finish()
    rows_w0[1].finish()
    last = [finish(0)]
    sums[4].second()
    last.append(finish(1))
    for copy in last:
        copy.wait()


def on_device(hessian, right_side, mask, damping):
    rows, columns = right_side.shape
    n, width = GROUPS, columns // GROUPS

    def many(*shape, dtype=F32):
        return pltpu.VMEM((n, *shape, width), dtype)

    anywhere = pl.BlockSpec(memory_space=pl.ANY)
    return pl.pallas_call(
        kernel,
        out_shape=jax.ShapeDtypeStruct((rows, columns), F32),
        in_specs=[anywhere] * 3 + [pl.BlockSpec(memory_space=pltpu.SMEM)],
        out_specs=anywhere,
        scratch_shapes=[
            pltpu.VMEM((2, DEPTH, WIDTH), F32),
            pltpu.VMEM((ROWS, WIDTH), BF16),
            pltpu.VMEM((ROWS, WIDTH), BF16),
            many(ROWS, dtype=jnp.int32),
            many(ROWS), many(ROWS), many(ROWS), many(WIDTH), many(WIDTH),
            many(WIDTH), many(ROWS),
            many(2, SHARD), many(5, SHARD), many(2, SHARD), many(5, SHARD), many(WIDTH),
            pltpu.VMEM((SHARD, columns), F32), pltpu.VMEM((SHARD, columns), jnp.int32), many(SHARD),
            many(WIDTH, dtype=BF16), many(WIDTH, dtype=BF16),
            pltpu.VMEM((SUMS, 2, 8, 128), F32),
            pltpu.VMEM((SUMS, NEAR + FAR, 8, 128), F32),
            pltpu.SemaphoreType.DMA((2,)),
            pltpu.SemaphoreType.DMA((2 * n,)),
            pltpu.SemaphoreType.DMA((n,)),
            pltpu.SemaphoreType.DMA((n, COPIES)),
            pltpu.SemaphoreType.DMA((n, COPIES)),
            pltpu.SemaphoreType.DMA((SUMS, NEAR + FAR)),
            pltpu.SemaphoreType.DMA((SUMS, NEAR + FAR)),
        ],
        compiler_params=pltpu.CompilerParams(
            collective_id=0, has_side_effects=True, vmem_limit_bytes=63 << 20
        ),
    )(hessian, right_side, mask, damping)


def solution(mesh):
    in_specs = (P("row", "col"), P("row", None), P("row", None), P())
    return jax.shard_map(
        on_device, mesh=mesh, in_specs=in_specs, out_specs=P("row", None), check_vma=False
    )
```

```python
import jax
import jax.numpy as jnp
from jax import lax
from jax.experimental import pallas as pl
from jax.experimental.pallas import tpu as pltpu
from jax.sharding import PartitionSpec as P

MESH = pl.DeviceIdType.MESH
F32 = jnp.float32
BF16 = jnp.bfloat16

epsilon = 1e-06

SHARD = 144
QUARTER = 2 * SHARD
WIDTH = 8 * SHARD
ROWS = 16 * SHARD
BLOCK = 4 * SHARD
DEPTH = 256
DEPTHS = ROWS // DEPTH
GROUPS = 2
COPIES = 48
SUMS = 5
NEAR = 7
FAR = 15


def halves(value):
    high = value.astype(BF16)
    return high, (value - high.astype(F32)).astype(BF16)


def dot3(a_high, a_low, b_high, b_low, contract):
    dims = ((contract, (0,)), ((), ()))

    def one(a, b):
        return lax.dot_general(a, b, dims, preferred_element_type=F32)

    return one(a_high, b_high) + (one(a_high, b_low) + one(a_low, b_high))


def column_sum(a, b):
    return jnp.sum(a * b, axis=0, keepdims=True)


class Copies:
    def __init__(self, send, receive):
        self.send, self.receive, self.used = send, receive, 0

    def to(self, source, target, device):
        k = self.used
        self.used += 1
        copy = pltpu.make_async_remote_copy(
            src_ref=source,
            dst_ref=target,
            send_sem=self.send.at[k],
            recv_sem=self.receive.at[k],
            device_id=device,
            device_id_type=MESH,
        )
        copy.start()
        return copy


class ToTwin:
    def __init__(self, copies, source, target, device, alone):
        k = copies.used
        copies.used += 1
        self.alone = alone
        self.remote = pltpu.make_async_remote_copy(
            src_ref=source,
            dst_ref=target,
            send_sem=copies.send.at[k],
            recv_sem=copies.receive.at[k],
            device_id=device,
            device_id_type=MESH,
        )
        self.local = pltpu.make_async_copy(source, target, copies.receive.at[k])

        @pl.when(self.alone)
        def _():
            self.local.start()

        @pl.when(jnp.logical_not(self.alone))
        def _():
            self.remote.start()

    def wait(self):
        @pl.when(self.alone)
        def _():
            self.local.wait()

        @pl.when(jnp.logical_not(self.alone))
        def _():
            self.remote.wait()


def shard_at(start, ring, half):
    return pl.ds(pl.multiple_of(start + ring * QUARTER + half * SHARD, 8), SHARD)


class Reduce:
    def __init__(self, copies, part, relay, got, start, ring, half, device):
        self.copies, self.part, self.relay, self.got = copies, part, relay, got
        self.start, self.ring, self.half, self.device = start, ring, half, device

    def shard(self, step, flip):
        half = 1 - self.half if flip else self.half
        return shard_at(self.start, lax.rem(self.ring + step, 4), half)

    def send(self, step, flip, slot):
        at = self.shard(step, flip)
        return self.copies.to(self.part.at[at, :], self.got.at[slot], self.device(step, flip))

    def first(self):
        up = self.copies.to(self.part.at[self.shard(2, False), :], self.relay.at[0], self.device(1, False))
        down = self.copies.to(self.part.at[self.shard(2, True), :], self.relay.at[1], self.device(3, False))
        self.relays = [up, down]
        self.sent = [self.send(1, True, 1), self.send(3, False, 2), self.send(0, True, 4)]

    def second(self):
        for k, (step, flip) in enumerate(((1, False), (3, True))):
            self.relays[k].wait()
            at = self.shard(step, flip)
            self.part[at, :] = self.part[at, :] + self.relay[k]
            self.sent.append(self.send(step, flip, 3 * k))

    def total(self):
        for copy in self.sent:
            copy.wait()
        got = self.got
        own = self.part[self.shard(0, False), :]
        return ((own + got[0]) + (got[1] + got[2])) + (got[3] + got[4])


class Gather:
    def __init__(self, copies, whole, start, ring, half, device):
        self.copies, self.whole, self.start = copies, whole, start
        self.ring, self.half, self.device = ring, half, device

    def send(self, at, step, flip):
        return self.copies.to(self.whole.at[at, :], self.whole.at[at, :], self.device(step, flip))

    def own(self):
        return shard_at(self.start, self.ring, self.half)

    def forward(self, below, above):
        at = shard_at(self.start, lax.rem(self.ring + 3, 4), self.half)
        below.wait_recv()
        up = self.send(at, 1, False)
        at = shard_at(self.start, lax.rem(self.ring + 1, 4), 1 - self.half)
        above.wait_recv()
        self.last = [up, self.send(at, 3, False)]

    def first(self):
        ways = ((1, False), (3, True), (1, True), (3, False), (0, True))
        self.sent = [self.send(self.own(), *way) for way in ways]

    def second(self):
        self.forward(self.sent[0], self.sent[1])

    def finish(self):
        for copy in self.last:
            copy.wait()
        for k, copy in enumerate(self.sent):
            if k < 2:
                copy.wait_send()
            else:
                copy.wait()


class GatherByAxis(Gather):
    def pair(self):
        self.across = self.send(self.own(), 0, True)

    def first(self):
        self.across.wait()
        at = pl.ds(pl.multiple_of(self.start + self.ring * QUARTER, 8), QUARTER)
        self.sent = [self.send(at, 1, False), self.send(at, 3, False)]

    def swap(self, core_peer):
        for copy in self.last:
            copy.wait()
        for copy in self.sent:
            copy.wait_send()
        at = pl.ds(self.start, WIDTH)
        self.half_sent = self.copies.to(self.whole.at[at, :], self.whole.at[at, :], core_peer)

    def finish(self):
        self.half_sent.wait()


class AllSums:
    def __init__(self, tile_out, tile_in, send, receive, place):
        self.tile_out, self.tile_in, self.copies = tile_out, tile_in, Copies(send, receive)
        self.near, self.far = place["near"], place["far"]

    def first(self, lines):
        self.tile_out[0] = jnp.zeros((8, 128), F32)
        for k, line in enumerate(lines):
            self.tile_out[0, pl.ds(k, 1), :] = line
        self.send(0, self.near)

    def send(self, step, peers):
        self.sent = []
        for peer in peers:
            k = self.copies.used
            self.sent.append(self.copies.to(self.tile_out.at[step], self.tile_in.at[k], peer))

    def added(self, step):
        for copy in self.sent:
            copy.wait()
        total = self.tile_out[step]
        for k in range(self.copies.used - len(self.sent), self.copies.used):
            total = total + self.tile_in[k]
        return total

    def second(self):
        self.tile_out[1] = self.added(0)
        self.send(1, self.far)

    def total(self):
        return self.added(1)


def lines_of(value):
    return [value[:, k * 128:(k + 1) * 128] for k in range(value.shape[1] // 128)]


def value_of(tile, first, count):
    return jnp.concatenate([tile[k:k + 1, :] for k in range(first, first + count)], axis=1)


def find_place():
    row, col = lax.axis_index("row"), lax.axis_index("col")
    x_low, z = lax.div(row, 4), lax.rem(row, 4)
    x_high, y, core = lax.div(col, 8), lax.rem(lax.div(col, 2), 4), lax.rem(col, 2)
    place = dict(x_low=x_low, z=z, x_high=x_high, y=y, core=core)

    def device(dz=0, dy=0, low=0, high=0, dcore=0):
        at_z, at_y = lax.rem(z + dz, 4), lax.rem(y + dy, 4)
        at_low = 1 - x_low if low else x_low
        at_high = 1 - x_high if high else x_high
        at_core = 1 - core if dcore else core
        return (at_low * 4 + at_z, at_high * 8 + at_y * 2 + at_core)

    place["on_row"] = lambda step, flip: device(dz=step, low=flip)
    place["on_col"] = lambda step, flip: device(dy=step, high=flip)
    place["core_peer"] = device(dcore=1)
    place["near"] = [
        device(low=a, high=b, dcore=c) for a in (0, 1) for b in (0, 1) for c in (0, 1) if a + b + c
    ]
    place["far"] = [device(dz=a, dy=b) for a in range(4) for b in range(4) if a + b]
    place["other"] = [device(dz=d, low=1) for d in (1, 3)] + [device(dy=d, high=1) for d in (1, 3)]
    ring, half = lax.rem(z + core, 4), lax.rem(x_low + core, 2)
    place["ring"], place["half"] = ring, half
    to_half = lax.rem(x_high + core, 2)

    place["to_columns"] = (to_half * 4 + lax.rem(y + 4 - core, 4), x_low * 8 + z * 2 + core)
    place["to_rows"] = (x_high * 4 + y, half * 8 + ring * 2 + core)
    place["alone"] = jnp.logical_and(jnp.logical_and(x_low == x_high, z == y), core == 0)
    return place


def kernel(
    h_hbm, b_hbm, mask_hbm, damping_ref, out_hbm,
    h_stage, h_high, h_low, mask, r0, w0_rows, r2_rows, cols1, cols2,
    part0, part1, relay0, got0, relay1, got1, got_core,
    b_own, mask_own, mask_sent,
    v_high, v_low, tile_out, tile_in, stage_sem, in_sem, out_sem, send_sem, receive_sem,
    sums_send, sums_receive,
):
    groups, _, width = r0.shape
    place = find_place()
    z, y, core, x_low, x_high = (place[k] for k in ("z", "y", "core", "x_low", "x_high"))
    core_peer = place["core_peer"]
    damping = damping_ref[0]

    def load(k, slot):
        return pltpu.make_async_copy(
            h_hbm.at[pl.ds(k * DEPTH, DEPTH), :], h_stage.at[slot], stage_sem.at[slot]
        )

    loads = []
    for g in range(groups):
        columns = pl.ds(g * width, width)
        loads.append(
            (
                pltpu.make_async_copy(b_hbm.at[:, columns], r0.at[g], in_sem.at[2 * g]),
                pltpu.make_async_copy(mask_hbm.at[:, columns], mask.at[g], in_sem.at[2 * g + 1]),
            )
        )
    for copy in loads[0]:
        copy.start()
    load(0, 0).start()
    load(1, 1).start()

    barrier = pltpu.get_barrier_semaphore()
    peers = [*place["near"], *place["far"], *place["other"]]
    for peer in peers:
        pl.semaphore_signal(barrier, inc=1, device_id=peer, device_id_type=MESH)

    @pl.when(jnp.logical_not(place["alone"]))
    def _():
        for peer in (place["to_rows"], place["to_columns"]):
            pl.semaphore_signal(barrier, inc=1, device_id=peer, device_id_type=MESH)

    mine, others = pl.multiple_of(core * WIDTH, 8), pl.multiple_of((1 - core) * WIDTH, 8)
    ring, half = place["ring"], place["half"]
    row_own, col_own = shard_at(mine, y, x_high), shard_at(0, ring, half)
    twin_row, twin_col = shard_at(mine, ring, half), shard_at(0, y, x_high)
    alone = place["alone"]

    def first_rows(g):
        for copy in loads[g]:
            copy.wait()

        @pl.loop(0, 8)
        def _(k):
            at = pl.ds(pl.multiple_of(k * QUARTER, 8), QUARTER)
            r0[g, at, :] = r0[g, at, :] * mask[g, at, :].astype(F32)

        mask_sent[g] = mask[g, row_own, :].astype(F32)

    def multiply_first(g, fresh):
        part0[g] = jnp.zeros_like(part0[g])

        @pl.loop(0, DEPTHS)
        def _(k):
            at = pl.ds(pl.multiple_of(k * DEPTH, DEPTH), DEPTH)
            if fresh:
                slot = lax.rem(k, 2)
                load(k, slot).wait()
                high, low = halves(h_stage[slot])
                h_high[at, :] = high
                h_low[at, :] = low

                @pl.when(k < DEPTHS - 2)
                def _():
                    load(k + 2, slot).start()
            b_high, b_low = halves(r0[g, at, :])
            part0[g] += dot3(h_high[at, :], h_low[at, :], b_high, b_low, (0,))

    def split_columns(source, g):
        @pl.loop(0, 4)
        def _(k):
            at = pl.ds(pl.multiple_of(k * QUARTER, 16), QUARTER)
            high, low = halves(source[g, at, :])
            v_high[g, at, :] = high
            v_low[g, at, :] = low

    def multiply_rows(at, g):
        return dot3(h_high[at, :], h_low[at, :], v_high[g], v_low[g], (1,))

    def multiply_block(g, half, k):
        at = pl.ds(pl.multiple_of(half + k * BLOCK, 16), BLOCK)
        part1[g, at, :] = multiply_rows(at, g)

    both = range(groups)
    copies = [Copies(send_sem.at[g], receive_sem.at[g]) for g in both]
    reduce_row = [
        Reduce(copies[g], part0.at[g], relay0.at[g], got0.at[g], 0, ring, half, place["on_row"]) for g in both
    ]
    reduce_col = [
        Reduce(copies[g], part1.at[g], relay1.at[g], got1.at[g], mine, y, x_high, place["on_col"]) for g in both
    ]
    gather_w0 = [Gather(copies[g], cols1.at[g], 0, ring, half, place["on_row"]) for g in both]
    gather_r2 = [Gather(copies[g], cols2.at[g], 0, ring, half, place["on_row"]) for g in both]
    rows_w0 = [GatherByAxis(copies[g], w0_rows.at[g], mine, y, x_high, place["on_col"]) for g in both]
    rows_r2 = [GatherByAxis(copies[g], r2_rows.at[g], mine, y, x_high, place["on_col"]) for g in both]
    sums = [
        AllSums(tile_out.at[s], tile_in.at[s], sums_send.at[s], sums_receive.at[s], place) for s in range(SUMS)
    ]
    lines = width // 128
    w0_moved, r2_moved, swaps, dots0 = {}, {}, {}, {}

    def end_first(g):
        summed = reduce_row[g].total()
        if g == 0:
            for copy in moved:
                copy.wait()
        columns = pl.ds(g * width, width)
        keep = mask_own[:, columns].astype(F32)
        r0_here = keep * b_own[:, columns]
        w0 = keep * (summed + damping * r0_here)
        cols1[g, col_own, :] = w0
        gather_w0[g].first()
        here, there = cols1.at[g, col_own, :], w0_rows.at[g, twin_row, :]
        w0_moved[g] = ToTwin(copies[g], here, there, place["to_rows"], alone)
        dots0[g] = (column_sum(r0_here, r0_here), column_sum(r0_here, w0))

    def send_other_half(g):
        swaps[g] = []
        pl.loop(0, 2)(lambda k: multiply_block(g, others, k))
        for k in range(2):
            at = pl.ds(pl.multiple_of(others + k * BLOCK, 16), BLOCK)
            inner = pl.ds(k * BLOCK, BLOCK)
            swaps[g].append(copies[g].to(part1.at[g, at, :], got_core.at[g, inner, :], core_peer))

    def add_other_core(g):
        for copy in swaps[g]:
            copy.wait()

        @pl.loop(0, 4)
        def _(k):
            at = pl.ds(pl.multiple_of(mine + k * QUARTER, 8), QUARTER)
            inner = pl.ds(pl.multiple_of(k * QUARTER, 8), QUARTER)
            part1[g, at, :] = part1[g, at, :] + got_core[g, inner, :]

        reduce_col[g].first()

    def sums_of(s, values):
        sums[s].first([line for value in values for line in lines_of(value)])

    shards = {}

    def end_second(g):
        summed = reduce_col[g].total()
        r0_here, w0 = r0[g, row_own, :], w0_rows[g, row_own, :]
        r1 = r0_here - step0[g] * w0
        w1 = w0 - step0[g] * (mask_sent[g] * (summed + damping * w0))
        r2_rows[g, row_own, :] = w1
        sums_of(1 + g, [column_sum(r1, r1), column_sum(r1, w1), column_sum(r1, w0)])

    def make_r2(g):
        tile = sums[1 + g].total()
        norm1, inner1, cross1 = (value_of(tile, k * lines, lines) for k in range(3))
        ratio0 = norm1 / (norm0[g] + epsilon)
        curve1 = inner1 + ratio0 * (2.0 * cross1 + ratio0 * curve0[g])
        step1 = norm1 / (curve1 + epsilon)
        w0 = w0_rows[g, row_own, :]
        along = r2_rows[g, row_own, :] + ratio0 * w0
        r2 = (r0[g, row_own, :] - step0[g] * w0) - step1 * along
        r2_rows[g, row_own, :] = r2
        here, there = r2_rows.at[g, row_own, :], cols2.at[g, twin_col, :]
        r2_moved[g] = ToTwin(copies[g], here, there, place["to_columns"], alone)
        rows_r2[g].pair()
        shards[g] = (norm1, ratio0, curve1, step1, column_sum(r2, r2), column_sum(r2, along))

    def dotted(g, half):
        def one(k, total):
            at = pl.ds(pl.multiple_of(half + k * BLOCK, 16), BLOCK)
            return total + column_sum(r2_rows[g, at, :], multiply_rows(at, g))

        return lax.fori_loop(0, 2, one, jnp.zeros((1, width), F32))

    def finish(g):
        tile = sums[3 + g].total()
        norm2, cross2, inner2 = (value_of(tile, k * lines, lines) for k in range(3))
        norm1, ratio0, curve1, step1, _, _ = shards[g]
        ratio1 = norm2 / (norm1 + epsilon)
        curve2 = (inner2 + damping * norm2) + ratio1 * (2.0 * cross2 + ratio1 * curve1)
        step2 = norm2 / (curve2 + epsilon)
        on_d1 = step1 + step2 * ratio1
        on_r0 = step0[g] + on_d1 * (1.0 + ratio0)
        on_w0 = on_d1 * step0[g]

        @pl.loop(0, 8)
        def _(k):
            at = pl.ds(pl.multiple_of(k * QUARTER, 8), QUARTER)
            r0[g, at, :] = (on_r0 * r0[g, at, :] - on_w0 * w0_rows[g, at, :]) + step2 * r2_rows[g, at, :]

        done = pltpu.make_async_copy(r0.at[g], out_hbm.at[:, pl.ds(g * width, width)], out_sem.at[g])
        done.start()
        return done

    @pl.when(jnp.logical_not(place["alone"]))
    def _():
        pl.semaphore_wait(barrier, len(peers) + 2)

    @pl.when(place["alone"])
    def _():
        pl.semaphore_wait(barrier, len(peers))

    moved = [
        ToTwin(copies[0], b_hbm.at[row_own, :], b_own, place["to_columns"], alone),
        ToTwin(copies[0], mask_hbm.at[row_own, :], mask_own, place["to_columns"], alone),
    ]
    first_rows(0)
    for copy in loads[1]:
        copy.start()
    multiply_first(0, True)
    reduce_row[0].first()
    first_rows(1)
    multiply_first(1, False)
    reduce_row[0].second()
    reduce_row[1].first()
    end_first(0)
    reduce_row[1].second()
    gather_w0[0].second()
    w0_moved[0].wait()
    rows_w0[0].pair()
    end_first(1)
    sums_of(0, [dots0[0][0], dots0[1][0], dots0[0][1], dots0[1][1]])
    rows_w0[0].first()
    gather_w0[0].finish()
    split_columns(cols1, 0)
    send_other_half(0)
    gather_w0[1].second()
    sums[0].second()
    w0_moved[1].wait()
    rows_w0[1].pair()
    rows_w0[0].forward(*rows_w0[0].sent)
    pl.loop(0, 2)(lambda k: multiply_block(0, mine, k))
    rows_w0[1].first()
    add_other_core(0)
    gather_w0[1].finish()
    split_columns(cols1, 1)
    send_other_half(1)
    reduce_col[0].second()
    tile = sums[0].total()
    norm0 = [value_of(tile, g * lines, lines) for g in both]
    curve0 = [value_of(tile, (2 + g) * lines, lines) for g in both]
    step0 = [norm0[g] / (curve0[g] + epsilon) for g in both]
    rows_w0[0].swap(core_peer)
    pl.loop(0, 2)(lambda k: multiply_block(1, mine, k))
    add_other_core(1)
    rows_w0[1].forward(*rows_w0[1].sent)
    end_second(0)
    reduce_col[1].second()
    sums[1].second()
    end_second(1)
    make_r2(0)
    sums[2].second()
    rows_r2[0].first()
    make_r2(1)
    r2_moved[0].wait()
    gather_r2[0].first()
    rows_r2[0].forward(*rows_r2[0].sent)
    rows_r2[1].first()
    r2_moved[1].wait()
    gather_r2[1].first()
    gather_r2[0].second()
    rows_r2[0].swap(core_peer)
    rows_r2[1].forward(*rows_r2[1].sent)
    gather_r2[0].finish()
    gather_r2[1].second()
    split_columns(cols2, 0)
    inner2 = dotted(0, mine)
    rows_r2[0].finish()
    rows_r2[1].swap(core_peer)
    rows_w0[1].swap(core_peer)
    sums_of(3, [*shards[0][4:], inner2 + dotted(0, others)])
    gather_r2[1].finish()
    split_columns(cols2, 1)
    sums[3].second()
    inner2 = dotted(1, mine)
    rows_r2[1].finish()
    sums_of(4, [*shards[1][4:], inner2 + dotted(1, others)])
    rows_w0[0].finish()
    rows_w0[1].finish()
    last = [finish(0)]
    sums[4].second()
    last.append(finish(1))
    for copy in last:
        copy.wait()


def on_device(hessian, right_side, mask, damping):
    rows, columns = right_side.shape
    n, width = GROUPS, columns // GROUPS

    def many(*shape, dtype=F32):
        return pltpu.VMEM((n, *shape, width), dtype)

    anywhere = pl.BlockSpec(memory_space=pl.ANY)
    return pl.pallas_call(
        kernel,
        out_shape=jax.ShapeDtypeStruct((rows, columns), F32),
        in_specs=[anywhere] * 3 + [pl.BlockSpec(memory_space=pltpu.SMEM)],
        out_specs=anywhere,
        scratch_shapes=[
            pltpu.VMEM((2, DEPTH, WIDTH), F32),
            pltpu.VMEM((ROWS, WIDTH), BF16),
            pltpu.VMEM((ROWS, WIDTH), BF16),
            many(ROWS, dtype=jnp.int32),
            many(ROWS), many(ROWS), many(ROWS), many(WIDTH), many(WIDTH),
            many(WIDTH), many(ROWS),
            many(2, SHARD), many(5, SHARD), many(2, SHARD), many(5, SHARD), many(WIDTH),
            pltpu.VMEM((SHARD, columns), F32), pltpu.VMEM((SHARD, columns), jnp.int32), many(SHARD),
            many(WIDTH, dtype=BF16), many(WIDTH, dtype=BF16),
            pltpu.VMEM((SUMS, 2, 8, 128), F32),
            pltpu.VMEM((SUMS, NEAR + FAR, 8, 128), F32),
            pltpu.SemaphoreType.DMA((2,)),
            pltpu.SemaphoreType.DMA((2 * n,)),
            pltpu.SemaphoreType.DMA((n,)),
            pltpu.SemaphoreType.DMA((n, COPIES)),
            pltpu.SemaphoreType.DMA((n, COPIES)),
            pltpu.SemaphoreType.DMA((SUMS, NEAR + FAR)),
            pltpu.SemaphoreType.DMA((SUMS, NEAR + FAR)),
        ],
        compiler_params=pltpu.CompilerParams(
            collective_id=0, has_side_effects=True, vmem_limit_bytes=63 << 20
        ),
    )(hessian, right_side, mask, damping)


def solution(mesh):
    in_specs = (P("row", "col"), P("row", None), P("row", None), P())
    return jax.shard_map(
        on_device, mesh=mesh, in_specs=in_specs, out_specs=P("row", None), check_vma=False
    )
```

```python
import jax
import jax.numpy as jnp
from jax import lax
from jax.experimental import pallas as pl
from jax.experimental.pallas import tpu as pltpu
from jax.sharding import PartitionSpec as P

MESH = pl.DeviceIdType.MESH
F32 = jnp.float32
BF16 = jnp.bfloat16

epsilon = 1e-06

SHARD = 144
QUARTER = 2 * SHARD
WIDTH = 8 * SHARD
ROWS = 16 * SHARD
BLOCK = 4 * SHARD
DEPTH = 256
DEPTHS = ROWS // DEPTH
GROUPS = 2
COPIES = 48
SUMS = 5
NEAR = 7
FAR = 15


def halves(value):
    high = value.astype(BF16)
    return high, (value - high.astype(F32)).astype(BF16)


def dot3(a_high, a_low, b_high, b_low, contract):
    dims = ((contract, (0,)), ((), ()))

    def one(a, b):
        return lax.dot_general(a, b, dims, preferred_element_type=F32)

    return one(a_high, b_high) + (one(a_high, b_low) + one(a_low, b_high))


def column_sum(a, b):
    return jnp.sum(a * b, axis=0, keepdims=True)


class Copies:
    def __init__(self, send, receive):
        self.send, self.receive, self.used = send, receive, 0

    def to(self, source, target, device):
        k = self.used
        self.used += 1
        copy = pltpu.make_async_remote_copy(
            src_ref=source,
            dst_ref=target,
            send_sem=self.send.at[k],
            recv_sem=self.receive.at[k],
            device_id=device,
            device_id_type=MESH,
        )
        copy.start()
        return copy


class ToTwin:
    def __init__(self, copies, source, target, device, alone):
        k = copies.used
        copies.used += 1
        self.alone = alone
        self.remote = pltpu.make_async_remote_copy(
            src_ref=source,
            dst_ref=target,
            send_sem=copies.send.at[k],
            recv_sem=copies.receive.at[k],
            device_id=device,
            device_id_type=MESH,
        )
        self.local = pltpu.make_async_copy(source, target, copies.receive.at[k])

        @pl.when(self.alone)
        def _():
            self.local.start()

        @pl.when(jnp.logical_not(self.alone))
        def _():
            self.remote.start()

    def wait(self):
        @pl.when(self.alone)
        def _():
            self.local.wait()

        @pl.when(jnp.logical_not(self.alone))
        def _():
            self.remote.wait()


def shard_at(start, ring, half):
    return pl.ds(pl.multiple_of(start + ring * QUARTER + half * SHARD, 8), SHARD)


class Reduce:
    def __init__(self, copies, part, relay, got, start, ring, half, device):
        self.copies, self.part, self.relay, self.got = copies, part, relay, got
        self.start, self.ring, self.half, self.device = start, ring, half, device

    def shard(self, step, flip):
        half = 1 - self.half if flip else self.half
        return shard_at(self.start, lax.rem(self.ring + step, 4), half)

    def send(self, step, flip, slot):
        at = self.shard(step, flip)
        return self.copies.to(self.part.at[at, :], self.got.at[slot], self.device(step, flip))

    def first(self):
        up = self.copies.to(self.part.at[self.shard(2, False), :], self.relay.at[0], self.device(1, False))
        down = self.copies.to(self.part.at[self.shard(2, True), :], self.relay.at[1], self.device(3, False))
        self.relays = [up, down]
        self.sent = [self.send(1, True, 1), self.send(3, False, 2), self.send(0, True, 4)]

    def second(self):
        for k, (step, flip) in enumerate(((1, False), (3, True))):
            self.relays[k].wait()
            at = self.shard(step, flip)
            self.part[at, :] = self.part[at, :] + self.relay[k]
            self.sent.append(self.send(step, flip, 3 * k))

    def total(self):
        for copy in self.sent:
            copy.wait()
        got = self.got
        own = self.part[self.shard(0, False), :]
        return ((own + got[0]) + (got[1] + got[2])) + (got[3] + got[4])


class Gather:
    def __init__(self, copies, whole, start, ring, half, device):
        self.copies, self.whole, self.start = copies, whole, start
        self.ring, self.half, self.device = ring, half, device

    def send(self, at, step, flip):
        return self.copies.to(self.whole.at[at, :], self.whole.at[at, :], self.device(step, flip))

    def own(self):
        return shard_at(self.start, self.ring, self.half)

    def forward(self, below, above):
        at = shard_at(self.start, lax.rem(self.ring + 3, 4), self.half)
        below.wait_recv()
        up = self.send(at, 1, False)
        at = shard_at(self.start, lax.rem(self.ring + 1, 4), 1 - self.half)
        above.wait_recv()
        self.last = [up, self.send(at, 3, False)]

    def first(self):
        ways = ((1, False), (3, True), (1, True), (3, False), (0, True))
        self.sent = [self.send(self.own(), *way) for way in ways]

    def second(self):
        self.forward(self.sent[0], self.sent[1])

    def finish(self):
        for copy in self.last:
            copy.wait()
        for k, copy in enumerate(self.sent):
            if k < 2:
                copy.wait_send()
            else:
                copy.wait()


class GatherByAxis(Gather):
    def pair(self):
        self.across = self.send(self.own(), 0, True)

    def first(self):
        self.across.wait()
        at = pl.ds(pl.multiple_of(self.start + self.ring * QUARTER, 8), QUARTER)
        self.sent = [self.send(at, 1, False), self.send(at, 3, False)]

    def swap(self, core_peer):
        for copy in self.last:
            copy.wait()
        for copy in self.sent:
            copy.wait_send()
        at = pl.ds(self.start, WIDTH)
        self.half_sent = self.copies.to(self.whole.at[at, :], self.whole.at[at, :], core_peer)

    def finish(self):
        self.half_sent.wait()


class AllSums:
    def __init__(self, tile_out, tile_in, send, receive, place):
        self.tile_out, self.tile_in, self.copies = tile_out, tile_in, Copies(send, receive)
        self.near, self.far = place["near"], place["far"]

    def first(self, lines):
        self.tile_out[0] = jnp.zeros((8, 128), F32)
        for k, line in enumerate(lines):
            self.tile_out[0, pl.ds(k, 1), :] = line
        self.send(0, self.near)

    def send(self, step, peers):
        self.sent = []
        for peer in peers:
            k = self.copies.used
            self.sent.append(self.copies.to(self.tile_out.at[step], self.tile_in.at[k], peer))

    def added(self, step):
        for copy in self.sent:
            copy.wait()
        total = self.tile_out[step]
        for k in range(self.copies.used - len(self.sent), self.copies.used):
            total = total + self.tile_in[k]
        return total

    def second(self):
        self.tile_out[1] = self.added(0)
        self.send(1, self.far)

    def total(self):
        return self.added(1)


def lines_of(value):
    return [value[:, k * 128:(k + 1) * 128] for k in range(value.shape[1] // 128)]


def value_of(tile, first, count):
    return jnp.concatenate([tile[k:k + 1, :] for k in range(first, first + count)], axis=1)


def find_place():
    row, col = lax.axis_index("row"), lax.axis_index("col")
    x_low, z = lax.div(row, 4), lax.rem(row, 4)
    x_high, y, core = lax.div(col, 8), lax.rem(lax.div(col, 2), 4), lax.rem(col, 2)
    place = dict(x_low=x_low, z=z, x_high=x_high, y=y, core=core)

    def device(dz=0, dy=0, low=0, high=0, dcore=0):
        at_z, at_y = lax.rem(z + dz, 4), lax.rem(y + dy, 4)
        at_low = 1 - x_low if low else x_low
        at_high = 1 - x_high if high else x_high
        at_core = 1 - core if dcore else core
        return (at_low * 4 + at_z, at_high * 8 + at_y * 2 + at_core)

    place["on_row"] = lambda step, flip: device(dz=step, low=flip)
    place["on_col"] = lambda step, flip: device(dy=step, high=flip)
    place["core_peer"] = device(dcore=1)
    place["near"] = [
        device(low=a, high=b, dcore=c) for a in (0, 1) for b in (0, 1) for c in (0, 1) if a + b + c
    ]
    place["far"] = [device(dz=a, dy=b) for a in range(4) for b in range(4) if a + b]
    place["other"] = [device(dz=d, low=1) for d in (1, 3)] + [device(dy=d, high=1) for d in (1, 3)]
    ring, half = lax.rem(z + core, 4), lax.rem(x_low + core, 2)
    place["ring"], place["half"] = ring, half
    to_half = lax.rem(x_high + core, 2)

    place["to_columns"] = (to_half * 4 + lax.rem(y + 4 - core, 4), x_low * 8 + z * 2 + core)
    place["to_rows"] = (x_high * 4 + y, half * 8 + ring * 2 + core)
    place["alone"] = jnp.logical_and(jnp.logical_and(x_low == x_high, z == y), core == 0)
    return place


def kernel(
    h_hbm, b_hbm, mask_hbm, damping_ref, out_hbm,
    h_stage, h_high, h_low, mask, r0, w0_rows, r2_rows, cols1, cols2,
    part0, part1, relay0, got0, relay1, got1, got_core,
    mask_own, mask_sent,
    v_high, v_low, tile_out, tile_in, stage_sem, in_sem, out_sem, send_sem, receive_sem,
    sums_send, sums_receive,
):
    groups, _, width = r0.shape
    place = find_place()
    z, y, core, x_low, x_high = (place[k] for k in ("z", "y", "core", "x_low", "x_high"))
    core_peer = place["core_peer"]
    damping = damping_ref[0]

    def load(k, slot):
        return pltpu.make_async_copy(
            h_hbm.at[pl.ds(k * DEPTH, DEPTH), :], h_stage.at[slot], stage_sem.at[slot]
        )

    loads = []
    for g in range(groups):
        columns = pl.ds(g * width, width)
        loads.append(
            (
                pltpu.make_async_copy(b_hbm.at[:, columns], r0.at[g], in_sem.at[2 * g]),
                pltpu.make_async_copy(mask_hbm.at[:, columns], mask.at[g], in_sem.at[2 * g + 1]),
            )
        )
    for copy in loads[0]:
        copy.start()
    load(0, 0).start()
    load(1, 1).start()
    for copy in loads[1]:
        copy.start()

    barrier = pltpu.get_barrier_semaphore()
    peers = [*place["near"], *place["far"], *place["other"]]
    for peer in peers:
        pl.semaphore_signal(barrier, inc=1, device_id=peer, device_id_type=MESH)

    @pl.when(jnp.logical_not(place["alone"]))
    def _():
        for peer in (place["to_rows"], place["to_columns"]):
            pl.semaphore_signal(barrier, inc=1, device_id=peer, device_id_type=MESH)

    mine, others = pl.multiple_of(core * WIDTH, 8), pl.multiple_of((1 - core) * WIDTH, 8)
    ring, half = place["ring"], place["half"]
    row_own, col_own = shard_at(mine, y, x_high), shard_at(0, ring, half)
    twin_row, twin_col = shard_at(mine, ring, half), shard_at(0, y, x_high)
    alone = place["alone"]

    def first_rows(g):
        for copy in loads[g]:
            copy.wait()

        @pl.loop(0, 8)
        def _(k):
            at = pl.ds(pl.multiple_of(k * QUARTER, 8), QUARTER)
            r0[g, at, :] = r0[g, at, :] * mask[g, at, :].astype(F32)

        mask_sent[g] = mask[g, row_own, :].astype(F32)

    def multiply_first(g, fresh):
        part0[g] = jnp.zeros_like(part0[g])

        @pl.loop(0, DEPTHS)
        def _(k):
            at = pl.ds(pl.multiple_of(k * DEPTH, DEPTH), DEPTH)
            if fresh:
                slot = lax.rem(k, 2)
                load(k, slot).wait()
                high, low = halves(h_stage[slot])
                h_high[at, :] = high
                h_low[at, :] = low

                @pl.when(k < DEPTHS - 2)
                def _():
                    load(k + 2, slot).start()
            b_high, b_low = halves(r0[g, at, :])
            part0[g] += dot3(h_high[at, :], h_low[at, :], b_high, b_low, (0,))

    def split_columns(source, g):
        @pl.loop(0, 4)
        def _(k):
            at = pl.ds(pl.multiple_of(k * QUARTER, 16), QUARTER)
            high, low = halves(source[g, at, :])
            v_high[g, at, :] = high
            v_low[g, at, :] = low

    def multiply_rows(at, g):
        return dot3(h_high[at, :], h_low[at, :], v_high[g], v_low[g], (1,))

    def multiply_block(g, half, k):
        at = pl.ds(pl.multiple_of(half + k * BLOCK, 16), BLOCK)
        part1[g, at, :] = multiply_rows(at, g)

    both = range(groups)
    copies = [Copies(send_sem.at[g], receive_sem.at[g]) for g in both]
    reduce_row = [
        Reduce(copies[g], part0.at[g], relay0.at[g], got0.at[g], 0, ring, half, place["on_row"]) for g in both
    ]
    reduce_col = [
        Reduce(copies[g], part1.at[g], relay1.at[g], got1.at[g], mine, y, x_high, place["on_col"]) for g in both
    ]
    gather_w0 = [Gather(copies[g], cols1.at[g], 0, ring, half, place["on_row"]) for g in both]
    gather_r2 = [Gather(copies[g], cols2.at[g], 0, ring, half, place["on_row"]) for g in both]
    rows_w0 = [GatherByAxis(copies[g], w0_rows.at[g], mine, y, x_high, place["on_col"]) for g in both]
    rows_r2 = [GatherByAxis(copies[g], r2_rows.at[g], mine, y, x_high, place["on_col"]) for g in both]
    sums = [
        AllSums(tile_out.at[s], tile_in.at[s], sums_send.at[s], sums_receive.at[s], place) for s in range(SUMS)
    ]
    lines = width // 128
    w0_moved, r2_moved, swaps, dots0 = {}, {}, {}, {}

    def end_first(g):
        summed = reduce_row[g].total()
        if g == 0:
            for copy in moved:
                copy.wait()
        columns = pl.ds(g * width, width)
        cols1[g, col_own, :] = mask_own[:, columns].astype(F32) * summed
        gather_w0[g].first()
        here, there = cols1.at[g, col_own, :], w0_rows.at[g, twin_row, :]
        w0_moved[g] = ToTwin(copies[g], here, there, place["to_rows"], alone)

    def make_w0(g):
        r0_here = r0[g, row_own, :]
        return r0_here, w0_rows[g, row_own, :] + damping * r0_here

    def end_move(g):
        w0_moved[g].wait()
        r0_here, w0 = make_w0(g)
        dots0[g] = (column_sum(r0_here, r0_here), column_sum(r0_here, w0))
        rows_w0[g].pair()

    def send_other_half(g):
        swaps[g] = []
        pl.loop(0, 2)(lambda k: multiply_block(g, others, k))
        for k in range(2):
            at = pl.ds(pl.multiple_of(others + k * BLOCK, 16), BLOCK)
            inner = pl.ds(k * BLOCK, BLOCK)
            swaps[g].append(copies[g].to(part1.at[g, at, :], got_core.at[g, inner, :], core_peer))

    def add_other_core(g):
        for copy in swaps[g]:
            copy.wait()

        @pl.loop(0, 4)
        def _(k):
            at = pl.ds(pl.multiple_of(mine + k * QUARTER, 8), QUARTER)
            inner = pl.ds(pl.multiple_of(k * QUARTER, 8), QUARTER)
            part1[g, at, :] = part1[g, at, :] + got_core[g, inner, :]

        reduce_col[g].first()

    def sums_of(s, values):
        sums[s].first([line for value in values for line in lines_of(value)])

    shards = {}

    def end_second(g):
        summed = reduce_col[g].total()
        r0_here, w0 = make_w0(g)
        r1 = r0_here - step0[g] * w0
        again = mask_sent[g] * summed + damping * (w0_rows[g, row_own, :] + w0)
        w1 = w0 - step0[g] * again
        r2_rows[g, row_own, :] = w1
        sums_of(1 + g, [column_sum(r1, r1), column_sum(r1, w1), column_sum(r1, w0)])

    def make_r2(g):
        tile = sums[1 + g].total()
        norm1, inner1, cross1 = (value_of(tile, k * lines, lines) for k in range(3))
        ratio0 = norm1 / (norm0[g] + epsilon)
        curve1 = inner1 + ratio0 * (2.0 * cross1 + ratio0 * curve0[g])
        step1 = norm1 / (curve1 + epsilon)
        r0_here, w0 = make_w0(g)
        along = r2_rows[g, row_own, :] + ratio0 * w0
        r2 = (r0_here - step0[g] * w0) - step1 * along
        r2_rows[g, row_own, :] = r2
        here, there = r2_rows.at[g, row_own, :], cols2.at[g, twin_col, :]
        r2_moved[g] = ToTwin(copies[g], here, there, place["to_columns"], alone)
        rows_r2[g].pair()
        shards[g] = (norm1, ratio0, curve1, step1, column_sum(r2, r2), column_sum(r2, along))

    def dotted(g, half):
        def one(k, total):
            at = pl.ds(pl.multiple_of(half + k * BLOCK, 16), BLOCK)
            return total + column_sum(r2_rows[g, at, :], multiply_rows(at, g))

        return lax.fori_loop(0, 2, one, jnp.zeros((1, width), F32))

    def finish(g):
        tile = sums[3 + g].total()
        norm2, cross2, inner2 = (value_of(tile, k * lines, lines) for k in range(3))
        norm1, ratio0, curve1, step1, _, _ = shards[g]
        ratio1 = norm2 / (norm1 + epsilon)
        curve2 = (inner2 + damping * norm2) + ratio1 * (2.0 * cross2 + ratio1 * curve1)
        step2 = norm2 / (curve2 + epsilon)
        on_d1 = step1 + step2 * ratio1
        on_w0 = on_d1 * step0[g]
        on_r0 = step0[g] + on_d1 * (1.0 + ratio0) - on_w0 * damping

        @pl.loop(0, 8)
        def _(k):
            at = pl.ds(pl.multiple_of(k * QUARTER, 8), QUARTER)
            r0[g, at, :] = (on_r0 * r0[g, at, :] - on_w0 * w0_rows[g, at, :]) + step2 * r2_rows[g, at, :]

        done = pltpu.make_async_copy(r0.at[g], out_hbm.at[:, pl.ds(g * width, width)], out_sem.at[g])
        done.start()
        return done

    @pl.when(jnp.logical_not(place["alone"]))
    def _():
        pl.semaphore_wait(barrier, len(peers) + 2)

    @pl.when(place["alone"])
    def _():
        pl.semaphore_wait(barrier, len(peers))

    moved = [
        ToTwin(copies[0], mask_hbm.at[row_own, :], mask_own, place["to_columns"], alone),
    ]
    first_rows(0)
    multiply_first(0, True)
    reduce_row[0].first()
    first_rows(1)
    multiply_first(1, False)
    reduce_row[0].second()
    reduce_row[1].first()
    end_first(0)
    reduce_row[1].second()
    gather_w0[0].second()
    end_move(0)
    end_first(1)
    rows_w0[0].first()
    gather_w0[0].finish()
    split_columns(cols1, 0)
    send_other_half(0)
    gather_w0[1].second()
    rows_w0[0].forward(*rows_w0[0].sent)
    pl.loop(0, 2)(lambda k: multiply_block(0, mine, k))
    add_other_core(0)
    end_move(1)
    sums_of(0, [dots0[0][0], dots0[1][0], dots0[0][1], dots0[1][1]])
    gather_w0[1].finish()
    split_columns(cols1, 1)
    reduce_col[0].second()
    sums[0].second()
    rows_w0[1].first()
    send_other_half(1)
    rows_w0[0].swap(core_peer)
    pl.loop(0, 2)(lambda k: multiply_block(1, mine, k))
    add_other_core(1)
    tile = sums[0].total()
    norm0 = [value_of(tile, g * lines, lines) for g in both]
    curve0 = [value_of(tile, (2 + g) * lines, lines) for g in both]
    step0 = [norm0[g] / (curve0[g] + epsilon) for g in both]
    rows_w0[1].forward(*rows_w0[1].sent)
    end_second(0)
    reduce_col[1].second()
    sums[1].second()
    end_second(1)
    make_r2(0)
    sums[2].second()
    r2_moved[0].wait()
    gather_r2[0].first()
    rows_r2[0].first()
    make_r2(1)
    gather_r2[0].second()
    rows_r2[0].forward(*rows_r2[0].sent)
    rows_w0[1].swap(core_peer)
    r2_moved[1].wait()
    gather_r2[1].first()
    rows_r2[1].first()
    gather_r2[0].finish()
    rows_r2[0].swap(core_peer)
    split_columns(cols2, 0)
    inner2 = dotted(0, mine)
    gather_r2[1].second()
    rows_r2[1].forward(*rows_r2[1].sent)
    rows_r2[0].finish()
    sums_of(3, [*shards[0][4:], inner2 + dotted(0, others)])
    gather_r2[1].finish()
    rows_r2[1].swap(core_peer)
    split_columns(cols2, 1)
    sums[3].second()
    inner2 = dotted(1, mine)
    rows_r2[1].finish()
    sums_of(4, [*shards[1][4:], inner2 + dotted(1, others)])
    rows_w0[0].finish()
    rows_w0[1].finish()
    last = [finish(0)]
    sums[4].second()
    last.append(finish(1))
    for copy in last:
        copy.wait()


def on_device(hessian, right_side, mask, damping):
    rows, columns = right_side.shape
    n, width = GROUPS, columns // GROUPS

    def many(*shape, dtype=F32):
        return pltpu.VMEM((n, *shape, width), dtype)

    anywhere = pl.BlockSpec(memory_space=pl.ANY)
    return pl.pallas_call(
        kernel,
        out_shape=jax.ShapeDtypeStruct((rows, columns), F32),
        in_specs=[anywhere] * 3 + [pl.BlockSpec(memory_space=pltpu.SMEM)],
        out_specs=anywhere,
        scratch_shapes=[
            pltpu.VMEM((2, DEPTH, WIDTH), F32),
            pltpu.VMEM((ROWS, WIDTH), BF16),
            pltpu.VMEM((ROWS, WIDTH), BF16),
            many(ROWS, dtype=jnp.int32),
            many(ROWS), many(ROWS), many(ROWS), many(WIDTH), many(WIDTH),
            many(WIDTH), many(ROWS),
            many(2, SHARD), many(5, SHARD), many(2, SHARD), many(5, SHARD), many(WIDTH),
            pltpu.VMEM((SHARD, columns), jnp.int32), many(SHARD),
            many(WIDTH, dtype=BF16), many(WIDTH, dtype=BF16),
            pltpu.VMEM((SUMS, 2, 8, 128), F32),
            pltpu.VMEM((SUMS, NEAR + FAR, 8, 128), F32),
            pltpu.SemaphoreType.DMA((2,)),
            pltpu.SemaphoreType.DMA((2 * n,)),
            pltpu.SemaphoreType.DMA((n,)),
            pltpu.SemaphoreType.DMA((n, COPIES)),
            pltpu.SemaphoreType.DMA((n, COPIES)),
            pltpu.SemaphoreType.DMA((SUMS, NEAR + FAR)),
            pltpu.SemaphoreType.DMA((SUMS, NEAR + FAR)),
        ],
        compiler_params=pltpu.CompilerParams(
            collective_id=0, has_side_effects=True, vmem_limit_bytes=63 << 20
        ),
    )(hessian, right_side, mask, damping)


def solution(mesh):
    in_specs = (P("row", "col"), P("row", None), P("row", None), P())
    return jax.shard_map(
        on_device, mesh=mesh, in_specs=in_specs, out_specs=P("row", None), check_vma=False
    )
```

```python
import jax
import jax.numpy as jnp
from jax import lax
from jax.experimental import pallas as pl
from jax.experimental.pallas import tpu as pltpu
from jax.sharding import PartitionSpec as P

MESH = pl.DeviceIdType.MESH
F32 = jnp.float32
BF16 = jnp.bfloat16

epsilon = 1e-06

SHARD = 144
QUARTER = 2 * SHARD
WIDTH = 8 * SHARD
ROWS = 16 * SHARD
BLOCK = 4 * SHARD
DEPTH = 256
DEPTHS = ROWS // DEPTH
GROUPS = 2
COPIES = 48
SUMS = 5
NEAR = 7
FAR = 15


def halves(value):
    high = value.astype(BF16)
    return high, (value - high.astype(F32)).astype(BF16)


def dot3(a_high, a_low, b_high, b_low, contract):
    dims = ((contract, (0,)), ((), ()))

    def one(a, b):
        return lax.dot_general(a, b, dims, preferred_element_type=F32)

    return one(a_high, b_high) + (one(a_high, b_low) + one(a_low, b_high))


def column_sum(a, b):
    return jnp.sum(a * b, axis=0, keepdims=True)


class Copies:
    def __init__(self, send, receive):
        self.send, self.receive, self.used = send, receive, 0

    def to(self, source, target, device):
        k = self.used
        self.used += 1
        copy = pltpu.make_async_remote_copy(
            src_ref=source,
            dst_ref=target,
            send_sem=self.send.at[k],
            recv_sem=self.receive.at[k],
            device_id=device,
            device_id_type=MESH,
        )
        copy.start()
        return copy


class ToTwin:
    def __init__(self, copies, source, target, device, alone):
        k = copies.used
        copies.used += 1
        self.alone = alone
        self.remote = pltpu.make_async_remote_copy(
            src_ref=source,
            dst_ref=target,
            send_sem=copies.send.at[k],
            recv_sem=copies.receive.at[k],
            device_id=device,
            device_id_type=MESH,
        )
        self.local = pltpu.make_async_copy(source, target, copies.receive.at[k])

        @pl.when(self.alone)
        def _():
            self.local.start()

        @pl.when(jnp.logical_not(self.alone))
        def _():
            self.remote.start()

    def wait(self):
        @pl.when(self.alone)
        def _():
            self.local.wait()

        @pl.when(jnp.logical_not(self.alone))
        def _():
            self.remote.wait()


def shard_at(start, ring, half):
    return pl.ds(pl.multiple_of(start + ring * QUARTER + half * SHARD, 8), SHARD)


class Reduce:
    def __init__(self, copies, part, relay, got, start, ring, half, device):
        self.copies, self.part, self.relay, self.got = copies, part, relay, got
        self.start, self.ring, self.half, self.device = start, ring, half, device

    def shard(self, step, flip):
        half = 1 - self.half if flip else self.half
        return shard_at(self.start, lax.rem(self.ring + step, 4), half)

    def send(self, step, flip, slot):
        at = self.shard(step, flip)
        return self.copies.to(self.part.at[at, :], self.got.at[slot], self.device(step, flip))

    def first(self):
        up = self.copies.to(self.part.at[self.shard(2, False), :], self.relay.at[0], self.device(1, False))
        down = self.copies.to(self.part.at[self.shard(2, True), :], self.relay.at[1], self.device(3, False))
        self.relays = [up, down]
        self.sent = [self.send(1, True, 1), self.send(3, False, 2), self.send(0, True, 4)]

    def second(self):
        for k, (step, flip) in enumerate(((1, False), (3, True))):
            self.relays[k].wait()
            at = self.shard(step, flip)
            self.part[at, :] = self.part[at, :] + self.relay[k]
            self.sent.append(self.send(step, flip, 3 * k))

    def total(self):
        for copy in self.sent:
            copy.wait()
        got = self.got
        own = self.part[self.shard(0, False), :]
        return ((own + got[0]) + (got[1] + got[2])) + (got[3] + got[4])


class ReduceByAxis(Reduce):
    def send(self, step, flip, slot):
        at = self.shard(step, flip)
        return self.copies.to(self.part.at[at, :], self.got.at[slot], self.device(step, flip and step == 0))

    def first(self):
        up = self.copies.to(self.part.at[self.shard(2, False), :], self.relay.at[0], self.device(1, False))
        down = self.copies.to(self.part.at[self.shard(2, True), :], self.relay.at[1], self.device(3, False))
        self.relays = [up, down]
        self.sent = [self.send(1, True, 1), self.send(3, False, 2)]

    def third(self):
        for copy in self.sent:
            copy.wait()
        at = self.shard(0, True)
        self.part[at, :] = self.part[at, :] + (self.got[1] + self.got[3])
        self.last = self.send(0, True, 4)

    def total(self):
        own = self.part[self.shard(0, False), :] + (self.got[0] + self.got[2])
        self.last.wait()
        return own + self.got[4]


class Gather:
    def __init__(self, copies, whole, start, ring, half, device):
        self.copies, self.whole, self.start = copies, whole, start
        self.ring, self.half, self.device = ring, half, device

    def send(self, at, step, flip):
        return self.copies.to(self.whole.at[at, :], self.whole.at[at, :], self.device(step, flip))

    def own(self):
        return shard_at(self.start, self.ring, self.half)

    def forward(self, below, above):
        at = shard_at(self.start, lax.rem(self.ring + 3, 4), self.half)
        below.wait_recv()
        up = self.send(at, 1, False)
        at = shard_at(self.start, lax.rem(self.ring + 1, 4), 1 - self.half)
        above.wait_recv()
        self.last = [up, self.send(at, 3, False)]

    def first(self):
        ways = ((1, False), (3, True), (1, True), (3, False), (0, True))
        self.sent = [self.send(self.own(), *way) for way in ways]

    def second(self):
        self.forward(self.sent[0], self.sent[1])

    def finish(self):
        for copy in self.last:
            copy.wait()
        for k, copy in enumerate(self.sent):
            if k < 2:
                copy.wait_send()
            else:
                copy.wait()


class GatherByAxis(Gather):
    def pair(self):
        self.across = self.send(self.own(), 0, True)

    def first(self):
        self.across.wait()
        at = pl.ds(pl.multiple_of(self.start + self.ring * QUARTER, 8), QUARTER)
        self.sent = [self.send(at, 1, False), self.send(at, 3, False)]

    def swap(self, core_peer):
        for copy in self.last:
            copy.wait()
        for copy in self.sent:
            copy.wait_send()
        at = pl.ds(self.start, WIDTH)
        self.half_sent = self.copies.to(self.whole.at[at, :], self.whole.at[at, :], core_peer)

    def finish(self):
        self.half_sent.wait()


class AllSums:
    def __init__(self, tile_out, tile_in, send, receive, place):
        self.tile_out, self.tile_in, self.copies = tile_out, tile_in, Copies(send, receive)
        self.near, self.far = place["near"], place["far"]

    def first(self, lines):
        self.tile_out[0] = jnp.zeros((8, 128), F32)
        for k, line in enumerate(lines):
            self.tile_out[0, pl.ds(k, 1), :] = line
        self.send(0, self.near)

    def send(self, step, peers):
        self.sent = []
        for peer in peers:
            k = self.copies.used
            self.sent.append(self.copies.to(self.tile_out.at[step], self.tile_in.at[k], peer))

    def added(self, step):
        for copy in self.sent:
            copy.wait()
        total = self.tile_out[step]
        for k in range(self.copies.used - len(self.sent), self.copies.used):
            total = total + self.tile_in[k]
        return total

    def second(self):
        self.tile_out[1] = self.added(0)
        self.send(1, self.far)

    def total(self):
        return self.added(1)


def lines_of(value):
    return [value[:, k * 128:(k + 1) * 128] for k in range(value.shape[1] // 128)]


def value_of(tile, first, count):
    return jnp.concatenate([tile[k:k + 1, :] for k in range(first, first + count)], axis=1)


def find_place():
    row, col = lax.axis_index("row"), lax.axis_index("col")
    x_low, z = lax.div(row, 4), lax.rem(row, 4)
    x_high, y, core = lax.div(col, 8), lax.rem(lax.div(col, 2), 4), lax.rem(col, 2)
    place = dict(x_low=x_low, z=z, x_high=x_high, y=y, core=core)

    def device(dz=0, dy=0, low=0, high=0, dcore=0):
        at_z, at_y = lax.rem(z + dz, 4), lax.rem(y + dy, 4)
        at_low = 1 - x_low if low else x_low
        at_high = 1 - x_high if high else x_high
        at_core = 1 - core if dcore else core
        return (at_low * 4 + at_z, at_high * 8 + at_y * 2 + at_core)

    place["on_row"] = lambda step, flip: device(dz=step, low=flip)
    place["on_col"] = lambda step, flip: device(dy=step, high=flip)
    place["core_peer"] = device(dcore=1)
    place["near"] = [
        device(low=a, high=b, dcore=c) for a in (0, 1) for b in (0, 1) for c in (0, 1) if a + b + c
    ]
    place["far"] = [device(dz=a, dy=b) for a in range(4) for b in range(4) if a + b]
    place["other"] = [device(dz=d, low=1) for d in (1, 3)] + [device(dy=d, high=1) for d in (1, 3)]
    ring, half = lax.rem(z + core, 4), lax.rem(x_low + core, 2)
    place["ring"], place["half"] = ring, half
    to_half = lax.rem(x_high + core, 2)

    place["to_columns"] = (to_half * 4 + lax.rem(y + 4 - core, 4), x_low * 8 + z * 2 + core)
    place["to_rows"] = (x_high * 4 + y, half * 8 + ring * 2 + core)
    place["alone"] = jnp.logical_and(jnp.logical_and(x_low == x_high, z == y), core == 0)
    return place


def kernel(
    h_hbm, b_hbm, mask_hbm, damping_ref, out_hbm,
    h_stage, h_high, h_low, mask, r0, w0_rows, r2_rows, cols1, cols2,
    part0, part1, relay0, got0, relay1, got1, got_core,
    mask_own, mask_sent,
    v_high, v_low, tile_out, tile_in, stage_sem, in_sem, out_sem, send_sem, receive_sem,
    sums_send, sums_receive,
):
    groups, _, width = r0.shape
    place = find_place()
    z, y, core, x_low, x_high = (place[k] for k in ("z", "y", "core", "x_low", "x_high"))
    core_peer = place["core_peer"]
    damping = damping_ref[0]

    def load(k, slot):
        return pltpu.make_async_copy(
            h_hbm.at[pl.ds(k * DEPTH, DEPTH), :], h_stage.at[slot], stage_sem.at[slot]
        )

    loads = []
    for g in range(groups):
        columns = pl.ds(g * width, width)
        loads.append(
            (
                pltpu.make_async_copy(b_hbm.at[:, columns], r0.at[g], in_sem.at[2 * g]),
                pltpu.make_async_copy(mask_hbm.at[:, columns], mask.at[g], in_sem.at[2 * g + 1]),
            )
        )
    for copy in loads[0]:
        copy.start()
    load(0, 0).start()
    load(1, 1).start()
    for copy in loads[1]:
        copy.start()

    barrier = pltpu.get_barrier_semaphore()
    peers = [*place["near"], *place["far"], *place["other"]]
    for peer in peers:
        pl.semaphore_signal(barrier, inc=1, device_id=peer, device_id_type=MESH)

    @pl.when(jnp.logical_not(place["alone"]))
    def _():
        for peer in (place["to_rows"], place["to_columns"]):
            pl.semaphore_signal(barrier, inc=1, device_id=peer, device_id_type=MESH)

    mine, others = pl.multiple_of(core * WIDTH, 8), pl.multiple_of((1 - core) * WIDTH, 8)
    ring, half = place["ring"], place["half"]
    row_own, col_own = shard_at(mine, y, x_high), shard_at(0, ring, half)
    twin_row, twin_col = shard_at(mine, ring, half), shard_at(0, y, x_high)
    alone = place["alone"]

    def first_rows(g):
        for copy in loads[g]:
            copy.wait()

        @pl.loop(0, 8)
        def _(k):
            at = pl.ds(pl.multiple_of(k * QUARTER, 8), QUARTER)
            r0[g, at, :] = r0[g, at, :] * mask[g, at, :].astype(F32)

        mask_sent[g] = mask[g, row_own, :].astype(F32)

    def multiply_first(g, fresh):
        part0[g] = jnp.zeros_like(part0[g])

        @pl.loop(0, DEPTHS)
        def _(k):
            at = pl.ds(pl.multiple_of(k * DEPTH, DEPTH), DEPTH)
            if fresh:
                slot = lax.rem(k, 2)
                load(k, slot).wait()
                high, low = halves(h_stage[slot])
                h_high[at, :] = high
                h_low[at, :] = low

                @pl.when(k < DEPTHS - 2)
                def _():
                    load(k + 2, slot).start()
            b_high, b_low = halves(r0[g, at, :])
            part0[g] += dot3(h_high[at, :], h_low[at, :], b_high, b_low, (0,))

    def split_columns(source, g):
        @pl.loop(0, 4)
        def _(k):
            at = pl.ds(pl.multiple_of(k * QUARTER, 16), QUARTER)
            high, low = halves(source[g, at, :])
            v_high[g, at, :] = high
            v_low[g, at, :] = low

    def multiply_rows(at, g):
        return dot3(h_high[at, :], h_low[at, :], v_high[g], v_low[g], (1,))

    def multiply_block(g, half, k):
        at = pl.ds(pl.multiple_of(half + k * BLOCK, 16), BLOCK)
        part1[g, at, :] = multiply_rows(at, g)

    both = range(groups)
    copies = [Copies(send_sem.at[g], receive_sem.at[g]) for g in both]
    reduce_row = [
        ReduceByAxis(copies[g], part0.at[g], relay0.at[g], got0.at[g], 0, ring, half, place["on_row"]) for g in both
    ]
    reduce_col = [
        ReduceByAxis(copies[g], part1.at[g], relay1.at[g], got1.at[g], mine, y, x_high, place["on_col"]) for g in both
    ]
    gather_w0 = [Gather(copies[g], cols1.at[g], 0, ring, half, place["on_row"]) for g in both]
    gather_r2 = [Gather(copies[g], cols2.at[g], 0, ring, half, place["on_row"]) for g in both]
    rows_w0 = [GatherByAxis(copies[g], w0_rows.at[g], mine, y, x_high, place["on_col"]) for g in both]
    rows_r2 = [GatherByAxis(copies[g], r2_rows.at[g], mine, y, x_high, place["on_col"]) for g in both]
    sums = [
        AllSums(tile_out.at[s], tile_in.at[s], sums_send.at[s], sums_receive.at[s], place) for s in range(SUMS)
    ]
    lines = width // 128
    w0_moved, r2_moved, swaps, dots0 = {}, {}, {}, {}

    def end_first(g):
        summed = reduce_row[g].total()
        if g == 0:
            for copy in moved:
                copy.wait()
        columns = pl.ds(g * width, width)
        cols1[g, col_own, :] = mask_own[:, columns].astype(F32) * summed
        gather_w0[g].first()
        here, there = cols1.at[g, col_own, :], w0_rows.at[g, twin_row, :]
        w0_moved[g] = ToTwin(copies[g], here, there, place["to_rows"], alone)

    def make_w0(g):
        r0_here = r0[g, row_own, :]
        return r0_here, w0_rows[g, row_own, :] + damping * r0_here

    def end_move(g):
        w0_moved[g].wait()
        r0_here, w0 = make_w0(g)
        dots0[g] = (column_sum(r0_here, r0_here), column_sum(r0_here, w0))
        rows_w0[g].pair()

    def send_other_half(g):
        swaps[g] = []
        pl.loop(0, 2)(lambda k: multiply_block(g, others, k))
        for k in range(2):
            at = pl.ds(pl.multiple_of(others + k * BLOCK, 16), BLOCK)
            inner = pl.ds(k * BLOCK, BLOCK)
            swaps[g].append(copies[g].to(part1.at[g, at, :], got_core.at[g, inner, :], core_peer))

    def add_other_core(g):
        for copy in swaps[g]:
            copy.wait()

        @pl.loop(0, 4)
        def _(k):
            at = pl.ds(pl.multiple_of(mine + k * QUARTER, 8), QUARTER)
            inner = pl.ds(pl.multiple_of(k * QUARTER, 8), QUARTER)
            part1[g, at, :] = part1[g, at, :] + got_core[g, inner, :]

        reduce_col[g].first()

    def sums_of(s, values):
        sums[s].first([line for value in values for line in lines_of(value)])

    shards = {}

    def end_second(g):
        summed = reduce_col[g].total()
        r0_here, w0 = make_w0(g)
        r1 = r0_here - step0[g] * w0
        again = mask_sent[g] * summed + damping * (w0_rows[g, row_own, :] + w0)
        w1 = w0 - step0[g] * again
        r2_rows[g, row_own, :] = w1
        sums_of(1 + g, [column_sum(r1, r1), column_sum(r1, w1), column_sum(r1, w0)])

    def make_r2(g):
        tile = sums[1 + g].total()
        norm1, inner1, cross1 = (value_of(tile, k * lines, lines) for k in range(3))
        ratio0 = norm1 / (norm0[g] + epsilon)
        curve1 = inner1 + ratio0 * (2.0 * cross1 + ratio0 * curve0[g])
        step1 = norm1 / (curve1 + epsilon)
        r0_here, w0 = make_w0(g)
        along = r2_rows[g, row_own, :] + ratio0 * w0
        r2 = (r0_here - step0[g] * w0) - step1 * along
        r2_rows[g, row_own, :] = r2
        here, there = r2_rows.at[g, row_own, :], cols2.at[g, twin_col, :]
        r2_moved[g] = ToTwin(copies[g], here, there, place["to_columns"], alone)
        rows_r2[g].pair()
        shards[g] = (norm1, ratio0, curve1, step1, column_sum(r2, r2), column_sum(r2, along))

    def dotted(g, half):
        def one(k, total):
            at = pl.ds(pl.multiple_of(half + k * BLOCK, 16), BLOCK)
            return total + column_sum(r2_rows[g, at, :], multiply_rows(at, g))

        return lax.fori_loop(0, 2, one, jnp.zeros((1, width), F32))

    def finish(g):
        tile = sums[3 + g].total()
        norm2, cross2, inner2 = (value_of(tile, k * lines, lines) for k in range(3))
        norm1, ratio0, curve1, step1, _, _ = shards[g]
        ratio1 = norm2 / (norm1 + epsilon)
        curve2 = (inner2 + damping * norm2) + ratio1 * (2.0 * cross2 + ratio1 * curve1)
        step2 = norm2 / (curve2 + epsilon)
        on_d1 = step1 + step2 * ratio1
        on_w0 = on_d1 * step0[g]
        on_r0 = step0[g] + on_d1 * (1.0 + ratio0) - on_w0 * damping

        @pl.loop(0, 8)
        def _(k):
            at = pl.ds(pl.multiple_of(k * QUARTER, 8), QUARTER)
            r0[g, at, :] = (on_r0 * r0[g, at, :] - on_w0 * w0_rows[g, at, :]) + step2 * r2_rows[g, at, :]

        done = pltpu.make_async_copy(r0.at[g], out_hbm.at[:, pl.ds(g * width, width)], out_sem.at[g])
        done.start()
        return done

    @pl.when(jnp.logical_not(place["alone"]))
    def _():
        pl.semaphore_wait(barrier, len(peers) + 2)

    @pl.when(place["alone"])
    def _():
        pl.semaphore_wait(barrier, len(peers))

    moved = [
        ToTwin(copies[0], mask_hbm.at[row_own, :], mask_own, place["to_columns"], alone),
    ]
    first_rows(0)
    multiply_first(0, True)
    reduce_row[0].first()
    first_rows(1)
    multiply_first(1, False)
    reduce_row[0].second()
    reduce_row[1].first()
    reduce_row[0].third()
    reduce_row[1].second()
    end_first(0)
    reduce_row[1].third()
    gather_w0[0].second()
    end_move(0)
    end_first(1)
    rows_w0[0].first()
    gather_w0[0].finish()
    split_columns(cols1, 0)
    send_other_half(0)
    gather_w0[1].second()
    rows_w0[0].forward(*rows_w0[0].sent)
    pl.loop(0, 2)(lambda k: multiply_block(0, mine, k))
    add_other_core(0)
    end_move(1)
    sums_of(0, [dots0[0][0], dots0[1][0], dots0[0][1], dots0[1][1]])
    gather_w0[1].finish()
    split_columns(cols1, 1)
    reduce_col[0].second()
    sums[0].second()
    rows_w0[1].first()
    send_other_half(1)
    rows_w0[0].swap(core_peer)
    pl.loop(0, 2)(lambda k: multiply_block(1, mine, k))
    add_other_core(1)
    tile = sums[0].total()
    norm0 = [value_of(tile, g * lines, lines) for g in both]
    curve0 = [value_of(tile, (2 + g) * lines, lines) for g in both]
    step0 = [norm0[g] / (curve0[g] + epsilon) for g in both]
    rows_w0[1].forward(*rows_w0[1].sent)
    reduce_col[0].third()
    reduce_col[1].second()
    end_second(0)
    reduce_col[1].third()
    sums[1].second()
    end_second(1)
    make_r2(0)
    sums[2].second()
    r2_moved[0].wait()
    gather_r2[0].first()
    rows_r2[0].first()
    make_r2(1)
    gather_r2[0].second()
    rows_r2[0].forward(*rows_r2[0].sent)
    rows_w0[1].swap(core_peer)
    r2_moved[1].wait()
    gather_r2[1].first()
    rows_r2[1].first()
    gather_r2[0].finish()
    rows_r2[0].swap(core_peer)
    split_columns(cols2, 0)
    inner2 = dotted(0, mine)
    gather_r2[1].second()
    rows_r2[1].forward(*rows_r2[1].sent)
    rows_r2[0].finish()
    sums_of(3, [*shards[0][4:], inner2 + dotted(0, others)])
    gather_r2[1].finish()
    rows_r2[1].swap(core_peer)
    split_columns(cols2, 1)
    sums[3].second()
    inner2 = dotted(1, mine)
    rows_r2[1].finish()
    sums_of(4, [*shards[1][4:], inner2 + dotted(1, others)])
    rows_w0[0].finish()
    rows_w0[1].finish()
    last = [finish(0)]
    sums[4].second()
    last.append(finish(1))
    for copy in last:
        copy.wait()


def on_device(hessian, right_side, mask, damping):
    rows, columns = right_side.shape
    n, width = GROUPS, columns // GROUPS

    def many(*shape, dtype=F32):
        return pltpu.VMEM((n, *shape, width), dtype)

    anywhere = pl.BlockSpec(memory_space=pl.ANY)
    return pl.pallas_call(
        kernel,
        out_shape=jax.ShapeDtypeStruct((rows, columns), F32),
        in_specs=[anywhere] * 3 + [pl.BlockSpec(memory_space=pltpu.SMEM)],
        out_specs=anywhere,
        scratch_shapes=[
            pltpu.VMEM((2, DEPTH, WIDTH), F32),
            pltpu.VMEM((ROWS, WIDTH), BF16),
            pltpu.VMEM((ROWS, WIDTH), BF16),
            many(ROWS, dtype=jnp.int32),
            many(ROWS), many(ROWS), many(ROWS), many(WIDTH), many(WIDTH),
            many(WIDTH), many(ROWS),
            many(2, SHARD), many(5, SHARD), many(2, SHARD), many(5, SHARD), many(WIDTH),
            pltpu.VMEM((SHARD, columns), jnp.int32), many(SHARD),
            many(WIDTH, dtype=BF16), many(WIDTH, dtype=BF16),
            pltpu.VMEM((SUMS, 2, 8, 128), F32),
            pltpu.VMEM((SUMS, NEAR + FAR, 8, 128), F32),
            pltpu.SemaphoreType.DMA((2,)),
            pltpu.SemaphoreType.DMA((2 * n,)),
            pltpu.SemaphoreType.DMA((n,)),
            pltpu.SemaphoreType.DMA((n, COPIES)),
            pltpu.SemaphoreType.DMA((n, COPIES)),
            pltpu.SemaphoreType.DMA((SUMS, NEAR + FAR)),
            pltpu.SemaphoreType.DMA((SUMS, NEAR + FAR)),
        ],
        compiler_params=pltpu.CompilerParams(
            collective_id=0, has_side_effects=True, vmem_limit_bytes=63 << 20
        ),
    )(hessian, right_side, mask, damping)


def solution(mesh):
    in_specs = (P("row", "col"), P("row", None), P("row", None), P())
    return jax.shard_map(
        on_device, mesh=mesh, in_specs=in_specs, out_specs=P("row", None), check_vma=False
    )
```
